128 devices in a mesh: sx: 8 (over x, z_hi), sy: 16 (over z_lo, y, core).
Axes of the slice: x: 4, y: 4, z: 4 (z_hi: 2, z_lo: 2; z = z_hi * 2 + z_lo), core: 2. Of those that a mesh axis runs over, the one named last changes fastest.
Arguments:
- scalar_field: float32 [256, 512, 512], P('sx', 'sy'), may hold values from -4 to 7
- diffusivity: float32 [256, 512, 512], P('sx', 'sy'), may hold values from 0.03 to 0.11
- reaction_rate: float32 [256, 512, 512], P('sx', 'sy'), may hold values from 0.05 to 0.5
- shear_offsets: int32 [4, 512], replicated, may hold values from 0 to 31
- depth_order: int32 [4, 512], replicated, may hold values from 0 to 1
- tf_centres: float32 [8], replicated, may hold values from -2 to 2
- tf_colour: float32 [3, 8], replicated, may hold values from 0.5 to 2
- tf_opacity: float32 [8], replicated, may hold values from 0.0009765625 to 0.009765625
Outputs:
- field_out: float32 [256, 512, 512], P('sx', 'sy')
- image: float32 [4, 3, 256, 512], P(None, None, ('sx', 'sy'))
- transmittance: float32 [4, 256, 512], P(None, ('sx', 'sy'))
The draws below stay inside these ranges and needn't reach their ends.
All inputs are finite; a program needn't handle non-finite values.
Results may differ from the reference program's by a relative error of at most 0.0002.
Values sent between devices are 32-bit elements; how exact they have to be, the bound alone decides.
No kernel may reach another device: no remote copies, remote signals or barrier semaphores. Data moves between devices by JAX's collectives and lax.ppermute only.
A program may use at most 128 MiB of HBM per device.

```python
import math
import jax
import jax.numpy as jnp
from jax import lax

CX = 32
NZ = 512
STEPS = 4
VIEWS = 4
BUMPS = 8
MAXSHIFT = 8
NX = 256
NY = 512


def draw_scalar_field(key, part):
    plane_key = jax.random.fold_in(key, 11)
    cell_key = jax.random.fold_in(key, 23)
    plane_shift = jax.random.uniform(plane_key, (NY,), jnp.float32, -1.5, 1.5)
    jitter_values = 0.8 * jax.random.normal(cell_key, (NX, NY, NZ), jnp.float32)
    return jnp.clip(plane_shift[None, :, None] + jitter_values, -4.0, 7.0)


def plant(entries, own_key, low, largest):
    dims = entries.shape
    index_at = [jax.random.randint(jax.random.fold_in(own_key, axis), (), 0, dims[axis]) for axis in range(len(dims))]
    entries = entries.at[tuple(index_at)].set(low)
    longest = dims.index(max(dims))
    index_at[longest] = (index_at[longest] + 1) % dims[longest]
    return entries.at[tuple(index_at)].set(largest)


def shard_levels(rng, dims, cuts, least, top_value):
    def one(axis_at, blocks):
        draws = jax.random.uniform(jax.random.fold_in(jax.random.fold_in(rng, 6), axis_at), (blocks,), jnp.float32, least / len(cuts), top_value / len(cuts))
        return jnp.repeat(jnp.exp(draws), dims[axis_at] // blocks).reshape((-1,) + (1,) * (len(dims) - axis_at - 1))

    loudness = one(*cuts[0])
    for cut in cuts[1:]:
        loudness = loudness * one(*cut)
    return loudness


def setup_inputs(seed: int = 0) -> dict:
    key_list = jax.random.split(jax.random.key(seed), 9)
    scalar_field = draw_scalar_field(jax.random.fold_in(key_list[8], 71), 0)
    diffusivity = jnp.clip(jnp.exp(math.log(0.11) - 1.299283 * jax.random.uniform(key_list[1], (NX, NY, NZ), jnp.float32) ** shard_levels(key_list[1], (NX, NY, NZ), ((0, 8), (1, 16)), -0.2, 0.2)), 0.03, 0.11)
    reaction_rate = jnp.clip(jnp.exp(math.log(0.5) - 2.3025851 * jax.random.uniform(key_list[2], (NX, NY, NZ), jnp.float32) ** shard_levels(key_list[2], (NX, NY, NZ), ((0, 8), (1, 16)), -0.2, 0.2)), 0.05, 0.5)
    shear_offsets = plant(jax.random.randint(key_list[3], (VIEWS, NY), 0, 4 * MAXSHIFT), jax.random.fold_in(key_list[3], 1), 0, (4 * MAXSHIFT) - 1).astype(jnp.int32)
    depth_order = plant(jax.random.randint(key_list[4], (VIEWS, NZ), 0, 2), jax.random.fold_in(key_list[4], 1), 0, 1).astype(jnp.int32)
    tf_centres = jnp.clip(jax.random.uniform(key_list[5], (BUMPS,), jnp.float32, -2.0, 2.0), -2.0, 2.0)
    tf_colour = jnp.clip(jnp.exp(jax.random.uniform(key_list[6], (3, BUMPS), jnp.float32, math.log(0.5), math.log(2.0))), 0.5, 2.0)
    tf_opacity = jnp.clip(jnp.exp(jax.random.uniform(key_list[7], (BUMPS,), jnp.float32, math.log(0.0009765625), math.log(0.009765625))), 0.0009765625, 0.009765625)
    return dict(scalar_field=scalar_field, diffusivity=diffusivity, reaction_rate=reaction_rate, shear_offsets=shear_offsets, depth_order=depth_order, tf_centres=tf_centres, tf_colour=tf_colour, tf_opacity=tf_opacity)


diff_gain = 0.4
bump_sharpness = 2.0


def neighbour_flux(field_pad, diff_pad):
    centre_cut = (slice(1, -1), slice(1, -1), slice(1, -1))
    neighbours = [
        (slice(2, None), slice(1, -1), slice(1, -1)),
        (slice(None, -2), slice(1, -1), slice(1, -1)),
        (slice(1, -1), slice(2, None), slice(1, -1)),
        (slice(1, -1), slice(None, -2), slice(1, -1)),
        (slice(1, -1), slice(1, -1), slice(2, None)),
        (slice(1, -1), slice(1, -1), slice(None, -2)),
    ]
    centre_field = field_pad[centre_cut]
    centre_diff = diff_pad[centre_cut]
    change = jnp.zeros_like(centre_field)
    for cut in neighbours:
        change = change + 0.5 * (centre_diff + diff_pad[cut]) * (field_pad[cut] - centre_field)
    return change


def shear_view(field_block, offsets):
    z_cells = field_block.shape[2]
    whole_cells = (offsets // 4).astype(jnp.int32)
    fraction = (offsets % 4).astype(jnp.float32) * 0.25
    padded = jnp.pad(field_block, ((0, 0), (0, 0), (0, MAXSHIFT + 1)))
    window = jax.vmap(lambda plane, start: lax.dynamic_slice_in_dim(plane, start, z_cells + 1, 1), in_axes=(1, 0), out_axes=1)(padded, whole_cells)
    fraction = fraction[None, :, None]
    return (1.0 - fraction) * window[:, :, :z_cells] + fraction * window[:, :, 1:]


def transfer(sheared, tf_centres, tf_colour, tf_opacity):
    optical = jnp.zeros_like(sheared)
    colours = [jnp.zeros_like(sheared) for channel in range(3)]
    for bump_index in range(tf_centres.shape[0]):
        bump_value = jnp.exp(-jnp.square(bump_sharpness * (sheared - tf_centres[bump_index])))
        optical = optical + tf_opacity[bump_index] * bump_value
        colours = [colours[channel] + tf_colour[channel, bump_index] * bump_value for channel in range(3)]
    return optical, colours


def render_block(field_block, shear_offsets, depth_order, tf_centres, tf_colour, tf_opacity):
    images = []
    lights = []
    for viewer in range(VIEWS):
        sheared = shear_view(field_block, shear_offsets[viewer])
        optical, colours = transfer(sheared, tf_centres, tf_colour, tf_opacity)
        running = jnp.cumsum(optical, axis=1)
        total = running[:, -1:, :]
        rising = (depth_order[viewer] == 0)[None, None, :]
        before = jnp.where(rising, running - optical, total - running)
        weight = (1.0 - jnp.exp(-optical)) * jnp.exp(-before)
        images.append(jnp.stack([jnp.sum(channel * weight, axis=1) for channel in colours]))
        lights.append(jnp.exp(-total[:, 0, :]))
    return jnp.stack(images), jnp.stack(lights)


def reference(scalar_field, diffusivity, reaction_rate, shear_offsets, depth_order, tf_centres, tf_colour, tf_opacity):
    field_now = scalar_field
    for iteration in range(STEPS):
        diff_now = diffusivity * (1.0 + diff_gain * jnp.tanh(field_now))
        change = neighbour_flux(jnp.pad(field_now, 1), jnp.pad(diff_now, 1))
        field_now = field_now + change + reaction_rate * jnp.tanh(field_now)
    blocks = field_now.reshape(NX // CX, CX, NY, NZ)
    images, lights = lax.map(lambda block: render_block(block, shear_offsets, depth_order, tf_centres, tf_colour, tf_opacity), blocks)
    image = jnp.transpose(images, (1, 2, 0, 3, 4)).reshape(VIEWS, 3, NX, NZ)
    transmittance = jnp.transpose(lights, (1, 0, 2, 3)).reshape(VIEWS, NX, NZ)
    return field_now, image, transmittance
```

```python
import functools

import jax
import jax.numpy as jnp
from jax import lax
from jax.experimental import pallas as pl
from jax.experimental.pallas import tpu as pltpu
from jax.sharding import PartitionSpec as P

STEPS = 4
VIEWS = 4
BUMPS = 8
W = STEPS
LOG2E = 1.4426950408889634
GAIN = 2.0 * LOG2E**0.5

F32 = jnp.float32


def shift(value, axis, up):
    size = lax.axis_size(axis)
    pairs = [(i, i + 1) for i in range(size - 1)]
    if not up:
        pairs = [(j, i) for i, j in pairs]
    return lax.ppermute(value, axis, pairs)


def stencil_kernel(
    place, u_hbm, d_hbm, r_hbm, xm_hbm, xp_hbm, yn, yp, cn, cp,
    out_hbm, ft_hbm,
    ua, ub, dd, rr, kbuf, fbuf, ft, sems, osem,
):
    cx, cy, nz = u_hbm.shape
    blocks = nz // 128
    tiles = cy // 8 + 1
    copies = []
    for src, dst in (
        (u_hbm, ua.at[W : W + cx, 0:cy]),
        (d_hbm, dd.at[W : W + cx, 0:cy]),
        (r_hbm, rr.at[W : W + cx, 0:cy]),
        (xm_hbm.at[0:W], ua.at[0:W, 0:cy]),
        (xm_hbm.at[W : 2 * W], dd.at[0:W, 0:cy]),
        (xm_hbm.at[2 * W : 3 * W - 1], rr.at[1:W, 0:cy]),
        (xp_hbm.at[0:W], ua.at[W + cx : 2 * W + cx, 0:cy]),
        (xp_hbm.at[W : 2 * W], dd.at[W + cx : 2 * W + cx, 0:cy]),
        (xp_hbm.at[2 * W : 3 * W - 1], rr.at[W + cx : 2 * W + cx - 1, 0:cy]),
    ):
        copies.append(pltpu.make_async_copy(src, dst, sems.at[len(copies)]))
    for copy in copies:
        copy.start()

    sx, sy = place[0], place[1]
    last_x, last_y = place[2] - 1, place[3] - 1

    def edge_rows(x, carry):
        for which, dst in enumerate((ua, dd, rr)):
            dst[W + x, cy : cy + W, :] = yn[which, x]
            dst[W + x, cy + W : cy + 2 * W, :] = yp[which, x]
        return carry

    lax.fori_loop(0, cx, edge_rows, 0)
    for side, base in ((0, 0), (1, W + cx)):
        for i in range(W):
            at = side * (3 * W - 1)
            for first, dst in ((0, ua), (W, dd)):
                dst[base + i, cy : cy + W, :] = cn[at + first + i]
                dst[base + i, cy + W : cy + 2 * W, :] = cp[at + first + i]
        for i in range(W - 1):
            at = side * (3 * W - 1) + 2 * W + i
            plane = base + i + (1 if side == 0 else 0)
            rr[plane, cy : cy + W, :] = cn[at]
            rr[plane, cy + W : cy + 2 * W, :] = cp[at]
    for i in range(W):
        ub[i] = jnp.zeros((cy + 8, nz), F32)
        ub[W + cx + i] = jnp.zeros((cy + 8, nz), F32)

    sub = lax.broadcasted_iota(jnp.int32, (8, 128), 0)
    lane = lax.broadcasted_iota(jnp.int32, (8, 128), 1)
    sub_last, sub_first = sub == 7, sub == 0
    lane_last, lane_first = lane == 127, lane == 0
    inside = jnp.where(sub < W, (sy < last_y).astype(F32), (sy > 0).astype(F32))

    for copy in copies:
        copy.wait()

    def cut(tile, block):
        return (slice(8 * tile, 8 * tile + 8), slice(128 * block, 128 * block + 128))

    def conductance(src, plane):
        slot = lax.rem(plane, 2)
        for t in range(tiles):
            for b in range(blocks):
                at = cut(t, b)
                kbuf[(slot,) + at] = dd[(plane,) + at] * (
                    0.5 + 0.2 * jnp.tanh(src[(plane,) + at])
                )

    def face(src, plane):
        slot = lax.rem(plane, 2)
        for t in range(tiles):
            for b in range(blocks):
                at = cut(t, b)
                fbuf[at] = (kbuf[(slot,) + at] + kbuf[(1 - slot,) + at]) * (
                    src[(plane,) + at] - src[(plane - 1,) + at]
                )

    def advance(src, dst, last, plane):
        conductance(src, plane + 1)
        slot = lax.rem(plane, 2)
        for b in range(blocks):
            u = [src[(plane,) + cut(t, b)] for t in range(tiles)]
            k = [kbuf[(slot,) + cut(t, b)] for t in range(tiles)]
            u_up = [pltpu.roll(v, 7, 0) for v in u]
            k_up = [pltpu.roll(v, 7, 0) for v in k]
            flux = []
            for t in range(tiles):
                n = (t + 1) % tiles
                un = jnp.where(sub_last, u_up[n], u_up[t])
                kn = jnp.where(sub_last, k_up[n], k_up[t])
                flux.append((k[t] + kn) * (un - u[t]))
            down = [pltpu.roll(v, 1, 0) for v in flux]
            for t in range(tiles - 1 if last else tiles):
                at = cut(t, b)
                change = flux[t] - jnp.where(sub_first, down[t - 1], down[t])
                ux = src[(plane + 1,) + at]
                kx = kbuf[(1 - slot,) + at]
                fx = (k[t] + kx) * (ux - u[t])
                change = change + (fx - fbuf[at])
                fbuf[at] = fx

                def z_face(low):
                    ul = src[(plane,) + cut(t, low)] if low != b else u[t]
                    kl = kbuf[(slot,) + cut(t, low)] if low != b else k[t]
                    un, kn = pltpu.roll(ul, 127, 1), pltpu.roll(kl, 127, 1)
                    if low + 1 < blocks:
                        u2 = pltpu.roll(src[(plane,) + cut(t, low + 1)], 127, 1)
                        k2 = pltpu.roll(kbuf[(slot,) + cut(t, low + 1)], 127, 1)
                    else:
                        u2 = k2 = jnp.zeros((8, 128), F32)
                    un, kn = jnp.where(lane_last, u2, un), jnp.where(lane_last, k2, kn)
                    return (kl + kn) * (un - ul)

                fz = z_face(b)
                rolled = pltpu.roll(fz, 1, 1)
                if b == 0:
                    carry = k[t] * u[t]
                else:
                    ul, kl = src[(plane,) + cut(t, b - 1)], kbuf[(slot,) + cut(t, b - 1)]
                    carry = (k[t] + pltpu.roll(kl, 1, 1)) * (u[t] - pltpu.roll(ul, 1, 1))
                change = change + (fz - jnp.where(lane_first, carry, rolled))
                new = u[t] + (change + rr[(plane,) + at] * jnp.tanh(u[t]))
                if t == tiles - 1:
                    new = new * inside
                if last:
                    dst[(plane - W,) + at] = new
                else:
                    dst[(plane,) + at] = new

    src, dst = ua, ub
    for step in range(STEPS):
        last = step == STEPS - 1
        low = jnp.where(sx == 0, W, step + 1)
        high = jnp.where(sx == last_x, W + cx, 2 * W + cx - 1 - step)
        if last:
            low, high = W, W + cx
        conductance(src, low - 1)
        conductance(src, low)
        face(src, low)

        def body(plane, carry, src=src, dst=ft if last else dst, last=last):
            advance(src, dst, last, plane)
            return carry

        lax.fori_loop(low, high, body, 0)
        if not last:
            src, dst = dst, src
    done = pltpu.make_async_copy(ft, out_hbm, osem.at[0])
    done.start()
    turned = dst

    def turn(xg, carry):
        for yg in range(cy // 8):
            for b in range(blocks):
                piece = ft[pl.ds(8 * xg, 8), 8 * yg : 8 * yg + 8, 128 * b : 128 * b + 128]
                turned[
                    8 * yg : 8 * yg + 8, pl.ds(pl.multiple_of(8 * xg, 8), 8), 128 * b : 128 * b + 128
                ] = jnp.transpose(piece, (1, 0, 2))
        return carry

    lax.fori_loop(0, cx // 8, turn, 0)
    move = pltpu.make_async_copy(turned.at[0:cy, 0:cx], ft_hbm, osem.at[1])
    move.start()
    done.wait()
    move.wait()


def stencil(place, u, d, r, xm, xp, yn, yp, cn, cp):
    cx, cy, nz = u.shape
    anywhere = pl.BlockSpec(memory_space=pl.ANY)
    local = pl.BlockSpec(memory_space=pltpu.VMEM)
    wide = (cx + 2 * W, cy + 8, nz)
    return pl.pallas_call(
        stencil_kernel,
        out_shape=(
            jax.ShapeDtypeStruct((cx, cy, nz), F32),
            jax.ShapeDtypeStruct((cy, cx, nz), F32),
        ),
        in_specs=[pl.BlockSpec(memory_space=pltpu.SMEM)] + [anywhere] * 5 + [local] * 4,
        out_specs=(anywhere, anywhere),
        scratch_shapes=[
            pltpu.VMEM(wide, F32),
            pltpu.VMEM(wide, F32),
            pltpu.VMEM(wide, F32),
            pltpu.VMEM(wide, F32),
            pltpu.VMEM((2, cy + 8, nz), F32),
            pltpu.VMEM((cy + 8, nz), F32),
            pltpu.VMEM((cx, cy, nz), F32),
            pltpu.SemaphoreType.DMA((9,)),
            pltpu.SemaphoreType.DMA((2,)),
        ],
        name="stencil",
    )(place, u, d, r, xm, xp, yn, yp, cn, cp)


def render_kernel(offs, cen, lev, mix, ft, sign_ref, out, sheared):
    view = pl.program_id(1)
    depth, rows, nz = ft.shape
    blocks = nz // 128
    lane = lax.broadcasted_iota(jnp.int32, (rows, 128), 1)
    lane_last = lane == 127
    zero = jnp.zeros((rows, 128), F32)

    def shear(y, carry):
        q = offs[view, y]
        whole = q // 4
        part = (q - 4 * whole).astype(F32) * 0.25
        cells = [ft[y, :, 128 * b : 128 * b + 128] for b in range(blocks)]
        back = [pltpu.roll(c, 127, 1) for c in cells] + [zero]
        mixed = []
        for b in range(blocks):
            after = jnp.where(lane_last, back[b + 1], back[b])
            mixed.append((cells[b] + part * (after - cells[b])) * GAIN)
        amount = lax.rem(128 - whole, 128)
        moved = [pltpu.roll(c, amount, 1) for c in mixed] + [zero]
        keep = lane < 128 - whole
        for b in range(blocks):
            sheared[y, :, 128 * b : 128 * b + 128] = jnp.where(keep, moved[b], moved[b + 1])
        return carry

    lax.fori_loop(0, depth, shear, 0, unroll=2)

    for b in range(blocks):
        at = slice(128 * b, 128 * b + 128)
        sign = jnp.broadcast_to(sign_ref[0, :, at], (rows, 128))
        rising = sign < 0.0
        light = jnp.ones((rows, 128), F32)
        sums = [zero] * BUMPS
        for y in range(depth):
            s = sheared[y, :, at]
            bumps = []
            for i in range(BUMPS):
                t = s - cen[i]
                bumps.append(jnp.exp2(lev[i] - t * t))
            pairs = [bumps[i] + bumps[i + 1] for i in range(0, BUMPS, 2)]
            total = (pairs[0] + pairs[1]) + (pairs[2] + pairs[3])
            after = light * jnp.exp2(total * sign)
            weight = light - after
            light = after
            sums = [sums[i] + bumps[i] * weight for i in range(BUMPS)]
        inverse = 1.0 / light
        through = jnp.where(rising, light, inverse)
        scale = jnp.where(rising, 1.0, -inverse)
        channels = []
        for c in range(3):
            value = mix[c, 0] * sums[0]
            for i in range(1, BUMPS):
                value = value + mix[c, i] * sums[i]
            channels.append(value * scale)
        channels.append(through)
        for d in range(rows // 2):
            out[d, :, at] = jnp.concatenate([c[2 * d : 2 * d + 2] for c in channels], axis=0)


def render(offs, cen, lev, mix, ft, signs):
    cy, cx, nz = ft.shape
    smem = pl.BlockSpec(memory_space=pltpu.SMEM)
    return pl.pallas_call(
        render_kernel,
        out_shape=jax.ShapeDtypeStruct((cx // 2, 8 * VIEWS, nz), F32),
        grid=(cx // 8, VIEWS),
        in_specs=[
            smem,
            smem,
            smem,
            smem,
            pl.BlockSpec((cy, 8, nz), lambda i, v: (0, i, 0)),
            pl.BlockSpec((1, 1, nz), lambda i, v: (v, 0, 0)),
        ],
        out_specs=pl.BlockSpec((4, 8, nz), lambda i, v: (i, v, 0)),
        scratch_shapes=[pltpu.VMEM((cy, 8, nz), F32)],
        name="render",
    )(offs, cen, lev, mix, ft, signs)


def combine_kernel(parts, sign_ref, image, trans):
    count, _, nz = parts.shape
    sub = lax.broadcasted_iota(jnp.int32, (8, nz), 0)
    for view in range(VIEWS):
        rising = jnp.broadcast_to(sign_ref[view], (8, nz)) < 0.0
        total = jnp.zeros((8, nz), F32)
        ahead = jnp.ones((8, nz), F32)
        for source in range(count):
            block = parts[source, 8 * view : 8 * view + 8, :]
            tail = jnp.where(sub >= 6, block, 0.0)
            pair = tail + pltpu.roll(tail, 4, 0)
            light = pair + pltpu.roll(pair, 2, 0)
            total = total * jnp.where(rising, 1.0, light) + block * jnp.where(rising, ahead, 1.0)
            ahead = ahead * light
        for c in range(3):
            image[view, c] = total[2 * c : 2 * c + 2]
        trans[view] = ahead[6:8]


def combine(parts, signs):
    nz = parts.shape[2]
    return pl.pallas_call(
        combine_kernel,
        out_shape=(
            jax.ShapeDtypeStruct((VIEWS, 3, 2, nz), F32),
            jax.ShapeDtypeStruct((VIEWS, 2, nz), F32),
        ),
        name="combine",
    )(parts, signs)


def per_device(u, d, r, offsets, depth_order, centres, colour, opacity):
    cx, cy, nz = u.shape
    place = jnp.stack(
        [
            lax.axis_index("sx"),
            lax.axis_index("sy"),
            jnp.int32(lax.axis_size("sx")),
            jnp.int32(lax.axis_size("sy")),
        ]
    ).astype(jnp.int32)
    up_x = jnp.concatenate([u[cx - W :], d[cx - W :], r[cx - W + 1 :]])
    down_x = jnp.concatenate([u[:W], d[:W], r[: W - 1]])
    xm = shift(up_x, "sx", True)
    xp = shift(down_x, "sx", False)
    up_y = jnp.stack([a[:, cy - W :] for a in (u, d, r)])
    down_y = jnp.stack([a[:, :W] for a in (u, d, r)])
    yp = shift(up_y, "sy", True)
    yn = shift(down_y, "sy", False)
    cp = shift(jnp.concatenate([xm[:, cy - W :], xp[:, cy - W :]]), "sy", True)
    cn = shift(jnp.concatenate([xm[:, :W], xp[:, :W]]), "sy", False)
    field, turned = stencil(place, u, d, r, xm, xp, yn, yp, cn, cp)

    offs = lax.dynamic_slice_in_dim(offsets, lax.axis_index("sy") * cy, cy, 1)
    signs = jnp.where(depth_order == 0, -1.0, 1.0).astype(F32)[:, None, :]
    level = opacity * LOG2E
    parts = render(offs, centres * GAIN, jnp.log2(level), colour / level, turned, signs)
    parts = lax.all_to_all(parts, "sy", split_axis=0, concat_axis=0, tiled=True)
    image, trans = combine(parts, signs)
    return field, image, trans


def solution(mesh):
    grid = P("sx", "sy", None)
    return jax.shard_map(
        per_device,
        mesh=mesh,
        in_specs=(grid, grid, grid, P(), P(), P(), P(), P()),
        out_specs=(
            grid,
            P(None, None, ("sx", "sy"), None),
            P(None, ("sx", "sy"), None),
        ),
        check_vma=False,
    )
```

```python
import functools

import jax
import jax.numpy as jnp
from jax import lax
from jax.experimental import pallas as pl
from jax.experimental.pallas import tpu as pltpu
from jax.sharding import PartitionSpec as P

STEPS = 4
VIEWS = 4
BUMPS = 8
MAXSHIFT = 8
W = STEPS
LOG2E = 1.4426950408889634
GAIN = 2.0 * LOG2E**0.5

F32 = jnp.float32


def shift(value, axis, up):
    size = lax.axis_size(axis)
    pairs = [(i, i + 1) for i in range(size - 1)]
    if not up:
        pairs = [(j, i) for i, j in pairs]
    return lax.ppermute(value, axis, pairs)


def stencil_kernel(
    place, u_hbm, d_hbm, r_hbm, xm_hbm, xp_hbm, yn, yp, cn, cp,
    out_hbm, ft_hbm,
    ua, ub, dd, rr, kk, fbuf, ft, sems, osem,
):
    cx, cy, nz = u_hbm.shape
    blocks = nz // 128
    tiles = cy // 8 + 1
    copies = []
    for src, dst in (
        (u_hbm, ua.at[W : W + cx, 0:cy]),
        (d_hbm, dd.at[W : W + cx, 0:cy]),
        (r_hbm, rr.at[W : W + cx, 0:cy]),
        (xm_hbm.at[0:W], ua.at[0:W, 0:cy]),
        (xm_hbm.at[W : 2 * W], dd.at[0:W, 0:cy]),
        (xm_hbm.at[2 * W : 3 * W - 1], rr.at[1:W, 0:cy]),
        (xp_hbm.at[0:W], ua.at[W + cx : 2 * W + cx, 0:cy]),
        (xp_hbm.at[W : 2 * W], dd.at[W + cx : 2 * W + cx, 0:cy]),
        (xp_hbm.at[2 * W : 3 * W - 1], rr.at[W + cx : 2 * W + cx - 1, 0:cy]),
    ):
        copies.append(pltpu.make_async_copy(src, dst, sems.at[len(copies)]))
    for copy in copies:
        copy.start()

    sx, sy = place[0], place[1]
    last_x, last_y = place[2] - 1, place[3] - 1

    def edge_rows(x, carry):
        for which, dst in enumerate((ua, dd, rr)):
            dst[W + x, cy : cy + W, :] = yn[which, x]
            dst[W + x, cy + W : cy + 2 * W, :] = yp[which, x]
        return carry

    lax.fori_loop(0, cx, edge_rows, 0)
    for side, base in ((0, 0), (1, W + cx)):
        for i in range(W):
            at = side * (3 * W - 1)
            for first, dst in ((0, ua), (W, dd)):
                dst[base + i, cy : cy + W, :] = cn[at + first + i]
                dst[base + i, cy + W : cy + 2 * W, :] = cp[at + first + i]
        for i in range(W - 1):
            at = side * (3 * W - 1) + 2 * W + i
            plane = base + i + (1 if side == 0 else 0)
            rr[plane, cy : cy + W, :] = cn[at]
            rr[plane, cy + W : cy + 2 * W, :] = cp[at]
    rr[0] = jnp.zeros((cy + 8, nz), F32)
    rr[2 * W + cx - 1] = jnp.zeros((cy + 8, nz), F32)
    zero = jnp.zeros((8, 128), F32)

    sub = lax.broadcasted_iota(jnp.int32, (8, 128), 0)
    lane = lax.broadcasted_iota(jnp.int32, (8, 128), 1)
    sub_last, sub_first = sub == 7, sub == 0
    lane_last, lane_first = lane == 127, lane == 0
    inside = jnp.where(sub < W, (sy < last_y).astype(F32), (sy > 0).astype(F32))

    for copy in copies:
        copy.wait()

    def cut(tile, block):
        return (slice(8 * tile, 8 * tile + 8), slice(128 * block, 128 * block + 128))

    def local_part(src, dst, plane):
        for t in range(tiles):
            u = [src[(plane,) + cut(t, b)] for b in range(blocks)]
            warm = [jnp.tanh(v) for v in u]
            k = [dd[(plane,) + cut(t, b)] * (0.5 + 0.2 * warm[b]) for b in range(blocks)]
            u_up = [pltpu.roll(v, 127, 1) for v in u] + [zero]
            k_up = [pltpu.roll(v, 127, 1) for v in k] + [zero]
            flux = []
            for b in range(blocks):
                un = jnp.where(lane_last, u_up[b + 1], u_up[b])
                kn = jnp.where(lane_last, k_up[b + 1], k_up[b])
                flux.append((k[b] + kn) * (un - u[b]))
            down = [pltpu.roll(v, 1, 1) for v in flux]
            for b in range(blocks):
                at = (plane,) + cut(t, b)
                low = jnp.where(lane_first, k[b] * u[b] if b == 0 else down[b - 1], down[b])
                kk[at] = k[b]
                dst[at] = u[b] + ((flux[b] - low) + rr[at] * warm[b])

    def across(src, base, dst, last, plane):
        for b in range(blocks):
            u = [src[(plane,) + cut(t, b)] for t in range(tiles)]
            k = [kk[(plane,) + cut(t, b)] for t in range(tiles)]
            u_up = [pltpu.roll(v, 7, 0) for v in u]
            k_up = [pltpu.roll(v, 7, 0) for v in k]
            flux = []
            for t in range(tiles):
                n = (t + 1) % tiles
                un = jnp.where(sub_last, u_up[n], u_up[t])
                kn = jnp.where(sub_last, k_up[n], k_up[t])
                flux.append((k[t] + kn) * (un - u[t]))
            down = [pltpu.roll(v, 1, 0) for v in flux]
            for t in range(tiles - 1 if last else tiles):
                at = cut(t, b)
                change = flux[t] - jnp.where(sub_first, down[t - 1], down[t])
                fx = (k[t] + kk[(plane + 1,) + at]) * (src[(plane + 1,) + at] - u[t])
                new = base[(plane,) + at] + (change + (fx - fbuf[at]))
                fbuf[at] = fx
                if t == tiles - 1:
                    new = new * inside
                dst[(plane - W if last else plane,) + at] = new

    def loop(low, count, fn):
        lax.fori_loop(0, count // 2, lambda i, c: (fn(low + 2 * i), fn(low + 2 * i + 1), c)[2], 0)

    src, dst = ua, ub
    for step in range(STEPS):
        last = step == STEPS - 1
        low, count = step + 1, cx + 2 * (W - 1 - step)
        loop(low - 1, count + 2, functools.partial(local_part, src, dst))
        for t in range(tiles):
            for b in range(blocks):
                at = cut(t, b)
                fbuf[at] = (kk[(low - 1,) + at] + kk[(low,) + at]) * (
                    src[(low,) + at] - src[(low - 1,) + at]
                )
        loop(low, count, functools.partial(across, src, dst, ft if last else dst, last))
        if not last:

            @pl.when(sx == 0)
            def _(dst=dst):
                for i in range(1, W):
                    dst[i] = jnp.zeros((cy + 8, nz), F32)

            @pl.when(sx == last_x)
            def _(dst=dst):
                for i in range(W - 1):
                    dst[W + cx + i] = jnp.zeros((cy + 8, nz), F32)

            src, dst = dst, src
    done = pltpu.make_async_copy(ft, out_hbm, osem.at[0])
    done.start()
    turned = dst

    def turn(xg, carry):
        for yg in range(cy // 8):
            for b in range(blocks):
                piece = ft[pl.ds(8 * xg, 8), 8 * yg : 8 * yg + 8, 128 * b : 128 * b + 128]
                turned[
                    8 * yg : 8 * yg + 8, pl.ds(pl.multiple_of(8 * xg, 8), 8), 128 * b : 128 * b + 128
                ] = jnp.transpose(piece, (1, 0, 2)) * GAIN
        return carry

    lax.fori_loop(0, cx // 8, turn, 0)
    move = pltpu.make_async_copy(turned.at[0:cy, 0:cx], ft_hbm, osem.at[1])
    move.start()
    done.wait()
    move.wait()


def stencil(place, u, d, r, xm, xp, yn, yp, cn, cp):
    cx, cy, nz = u.shape
    anywhere = pl.BlockSpec(memory_space=pl.ANY)
    local = pl.BlockSpec(memory_space=pltpu.VMEM)
    wide = (cx + 2 * W, cy + 8, nz)
    return pl.pallas_call(
        stencil_kernel,
        out_shape=(
            jax.ShapeDtypeStruct((cx, cy, nz), F32),
            jax.ShapeDtypeStruct((cy, cx, nz), F32),
        ),
        in_specs=[pl.BlockSpec(memory_space=pltpu.SMEM)] + [anywhere] * 5 + [local] * 4,
        out_specs=(anywhere, anywhere),
        scratch_shapes=[
            pltpu.VMEM(wide, F32),
            pltpu.VMEM(wide, F32),
            pltpu.VMEM(wide, F32),
            pltpu.VMEM(wide, F32),
            pltpu.VMEM(wide, F32),
            pltpu.VMEM((cy + 8, nz), F32),
            pltpu.VMEM((cx, cy, nz), F32),
            pltpu.SemaphoreType.DMA((9,)),
            pltpu.SemaphoreType.DMA((2,)),
        ],
        name="stencil",
    )(place, u, d, r, xm, xp, yn, yp, cn, cp)


def render_kernel(whole, part, cen, lev, mix, ft, sign_ref, out, moved):
    view = pl.program_id(1)
    depth, rows, nz = ft.shape
    blocks = nz // 128
    zero = jnp.zeros((rows, 128), F32)

    @pl.when(view == 0)
    def _():
        lane = lax.broadcasted_iota(jnp.int32, (rows, 128), 1)

        def shifts(y, carry):
            cells = [ft[y, :, 128 * b : 128 * b + 128] for b in range(blocks)]
            for b in range(blocks):
                moved[y, 0, :, 128 * b : 128 * b + 128] = cells[b]
            for n in range(1, MAXSHIFT + 1):
                back = [pltpu.roll(c, 128 - n, 1) for c in cells] + [zero]
                keep = lane < 128 - n
                for b in range(blocks):
                    moved[y, n, :, 128 * b : 128 * b + 128] = jnp.where(keep, back[b], back[b + 1])
            return carry

        lax.fori_loop(0, depth, shifts, 0, unroll=2)

    for b in range(blocks):
        at = slice(128 * b, 128 * b + 128)
        sign = jnp.broadcast_to(sign_ref[0, :, at], (rows, 128))
        rising = sign < 0.0
        light = jnp.ones((rows, 128), F32)
        sums = [zero] * BUMPS
        for y in range(depth):
            n = whole[view, y]
            near = moved[y, n, :, at]
            s = near + part[view, y] * (moved[y, n + 1, :, at] - near)
            bumps = []
            for i in range(BUMPS):
                t = s - cen[i]
                bumps.append(jnp.exp2(lev[i] - t * t))
            pairs = [bumps[i] + bumps[i + 1] for i in range(0, BUMPS, 2)]
            total = (pairs[0] + pairs[1]) + (pairs[2] + pairs[3])
            after = light * jnp.exp2(total * sign)
            weight = light - after
            light = after
            sums = [sums[i] + bumps[i] * weight for i in range(BUMPS)]
        inverse = 1.0 / light
        through = jnp.where(rising, light, inverse)
        scale = jnp.where(rising, 1.0, -inverse)
        channels = []
        for c in range(3):
            value = mix[c, 0] * sums[0]
            for i in range(1, BUMPS):
                value = value + mix[c, i] * sums[i]
            channels.append(value * scale)
        channels.append(through)
        for d in range(rows // 2):
            out[d, :, at] = jnp.concatenate([c[2 * d : 2 * d + 2] for c in channels], axis=0)


def render(whole, part, cen, lev, mix, ft, signs):
    cy, cx, nz = ft.shape
    smem = pl.BlockSpec(memory_space=pltpu.SMEM)
    return pl.pallas_call(
        render_kernel,
        out_shape=jax.ShapeDtypeStruct((cx // 2, 8 * VIEWS, nz), F32),
        grid=(cx // 8, VIEWS),
        in_specs=[
            smem,
            smem,
            smem,
            smem,
            smem,
            pl.BlockSpec((cy, 8, nz), lambda i, v: (0, i, 0)),
            pl.BlockSpec((1, 1, nz), lambda i, v: (v, 0, 0)),
        ],
        out_specs=pl.BlockSpec((4, 8, nz), lambda i, v: (i, v, 0)),
        scratch_shapes=[pltpu.VMEM((cy, MAXSHIFT + 1, 8, nz), F32)],
        name="render",
    )(whole, part, cen, lev, mix, ft, signs)


def combine_kernel(parts, sign_ref, image, trans):
    count, _, nz = parts.shape
    sub = lax.broadcasted_iota(jnp.int32, (8, nz), 0)
    for view in range(VIEWS):
        rising = jnp.broadcast_to(sign_ref[view], (8, nz)) < 0.0
        total = jnp.zeros((8, nz), F32)
        ahead = jnp.ones((8, nz), F32)
        for source in range(count):
            block = parts[source, 8 * view : 8 * view + 8, :]
            tail = jnp.where(sub >= 6, block, 0.0)
            pair = tail + pltpu.roll(tail, 4, 0)
            light = pair + pltpu.roll(pair, 2, 0)
            total = total * jnp.where(rising, 1.0, light) + block * jnp.where(rising, ahead, 1.0)
            ahead = ahead * light
        for c in range(3):
            image[view, c] = total[2 * c : 2 * c + 2]
        trans[view] = ahead[6:8]


def combine(parts, signs):
    nz = parts.shape[2]
    return pl.pallas_call(
        combine_kernel,
        out_shape=(
            jax.ShapeDtypeStruct((VIEWS, 3, 2, nz), F32),
            jax.ShapeDtypeStruct((VIEWS, 2, nz), F32),
        ),
        name="combine",
    )(parts, signs)


def per_device(u, d, r, offsets, depth_order, centres, colour, opacity):
    cx, cy, nz = u.shape
    place = jnp.stack(
        [
            lax.axis_index("sx"),
            lax.axis_index("sy"),
            jnp.int32(lax.axis_size("sx")),
            jnp.int32(lax.axis_size("sy")),
        ]
    ).astype(jnp.int32)
    up_x = jnp.concatenate([u[cx - W :], d[cx - W :], r[cx - W + 1 :]])
    down_x = jnp.concatenate([u[:W], d[:W], r[: W - 1]])
    xm = shift(up_x, "sx", True)
    xp = shift(down_x, "sx", False)
    up_y = jnp.stack([a[:, cy - W :] for a in (u, d, r)])
    down_y = jnp.stack([a[:, :W] for a in (u, d, r)])
    yp = shift(up_y, "sy", True)
    yn = shift(down_y, "sy", False)
    cp = shift(jnp.concatenate([xm[:, cy - W :], xp[:, cy - W :]]), "sy", True)
    cn = shift(jnp.concatenate([xm[:, :W], xp[:, :W]]), "sy", False)
    field, turned = stencil(place, u, d, r, xm, xp, yn, yp, cn, cp)

    offs = lax.dynamic_slice_in_dim(offsets, lax.axis_index("sy") * cy, cy, 1)
    signs = jnp.where(depth_order == 0, -1.0, 1.0).astype(F32)[:, None, :]
    level = opacity * LOG2E
    whole = offs // 4
    part = (offs % 4).astype(F32) * 0.25
    parts = render(whole, part, centres * GAIN, jnp.log2(level), colour / level, turned, signs)
    parts = lax.all_to_all(parts, "sy", split_axis=0, concat_axis=0, tiled=True)
    image, trans = combine(parts, signs)
    return field, image, trans


def solution(mesh):
    grid = P("sx", "sy", None)
    return jax.shard_map(
        per_device,
        mesh=mesh,
        in_specs=(grid, grid, grid, P(), P(), P(), P(), P()),
        out_specs=(
            grid,
            P(None, None, ("sx", "sy"), None),
            P(None, ("sx", "sy"), None),
        ),
        check_vma=False,
    )
```

```python
import jax
import jax.numpy as jnp
from jax import lax
from jax.experimental import pallas as pl
from jax.experimental.pallas import tpu as pltpu
from jax.sharding import PartitionSpec as P


STEPS = 4
VIEWS = 4
BUMPS = 8
MAXSHIFT = 8
W = STEPS
LOG2E = 1.4426950408889634
GAIN = 2.0 * LOG2E**0.5

F32 = jnp.float32


def shift(value, axis, up):
    size = lax.axis_size(axis)
    pairs = [(i, i + 1) for i in range(size - 1)]
    if not up:
        pairs = [(j, i) for i, j in pairs]
    return lax.ppermute(value, axis, pairs)


def cut(tile, block):
    return (slice(8 * tile, 8 * tile + 8), slice(128 * block, 128 * block + 128))


class Plane:
    def __init__(self, dd, rr, kk, fbuf, place):
        self.dd, self.rr, self.kk, self.fbuf = dd, rr, kk, fbuf
        self.tiles, self.blocks = dd.shape[1] // 8, dd.shape[2] // 128
        sub = lax.broadcasted_iota(jnp.int32, (8, 128), 0)
        lane = lax.broadcasted_iota(jnp.int32, (8, 128), 1)
        self.sub_last, self.sub_first = sub == 7, sub == 0
        self.lane_last, self.lane_first = lane == 127, lane == 0
        self.zero = jnp.zeros((8, 128), F32)
        self.inside = jnp.where(
            sub < W, (place[1] < place[3] - 1).astype(F32), (place[1] > 0).astype(F32)
        )

    def local(self, src, dst, plane):
        blocks = self.blocks
        for t in range(self.tiles):
            u = [src[(plane,) + cut(t, b)] for b in range(blocks)]
            warm = [jnp.tanh(v) for v in u]
            k = [self.dd[(plane,) + cut(t, b)] * (0.5 + 0.2 * warm[b]) for b in range(blocks)]
            u_up = [pltpu.roll(v, 127, 1) for v in u] + [self.zero]
            k_up = [pltpu.roll(v, 127, 1) for v in k] + [self.zero]
            flux = []
            for b in range(blocks):
                un = jnp.where(self.lane_last, u_up[b + 1], u_up[b])
                kn = jnp.where(self.lane_last, k_up[b + 1], k_up[b])
                flux.append((k[b] + kn) * (un - u[b]))
            down = [pltpu.roll(v, 1, 1) for v in flux]
            for b in range(blocks):
                at = (plane,) + cut(t, b)
                low = jnp.where(self.lane_first, k[b] * u[b] if b == 0 else down[b - 1], down[b])
                self.kk[at] = k[b]
                dst[at] = u[b] + ((flux[b] - low) + self.rr[at] * warm[b])

    def face(self, src, plane):
        for t in range(self.tiles):
            for b in range(self.blocks):
                at = cut(t, b)
                self.fbuf[at] = (self.kk[(plane - 1,) + at] + self.kk[(plane,) + at]) * (
                    src[(plane,) + at] - src[(plane - 1,) + at]
                )

    def across(self, src, base, dst, plane, target, keep=None):
        tiles, kk = self.tiles, self.kk
        for b in range(self.blocks):
            u = [src[(plane,) + cut(t, b)] for t in range(tiles)]
            k = [kk[(plane,) + cut(t, b)] for t in range(tiles)]
            u_up = [pltpu.roll(v, 7, 0) for v in u]
            k_up = [pltpu.roll(v, 7, 0) for v in k]
            flux = []
            for t in range(tiles):
                n = (t + 1) % tiles
                un = jnp.where(self.sub_last, u_up[n], u_up[t])
                kn = jnp.where(self.sub_last, k_up[n], k_up[t])
                flux.append((k[t] + kn) * (un - u[t]))
            down = [pltpu.roll(v, 1, 0) for v in flux]
            for t in range(min(tiles, dst.shape[1] // 8)):
                at = cut(t, b)
                change = flux[t] - jnp.where(self.sub_first, down[t - 1], down[t])
                fx = (k[t] + kk[(plane + 1,) + at]) * (src[(plane + 1,) + at] - u[t])
                new = base[(plane,) + at] + (change + (fx - self.fbuf[at]))
                self.fbuf[at] = fx
                if t == tiles - 1:
                    new = new * self.inside
                if keep is not None:
                    new = new * keep
                dst[(target,) + at] = new


def turn_over(field, turned):
    cx, cy, nz = field.shape[0], field.shape[1], field.shape[2]

    def group(xg, carry):
        rows = pl.ds(pl.multiple_of(8 * xg, 8), 8)
        for yg in range(cy // 8):
            for b in range(nz // 128):
                columns = slice(128 * b, 128 * b + 128)
                piece = field[rows, 8 * yg : 8 * yg + 8, columns]
                turned[8 * yg : 8 * yg + 8, rows, columns] = jnp.transpose(piece, (1, 0, 2)) * GAIN
        return carry

    lax.fori_loop(0, cx // 8, group, 0)


def inner_kernel(
    place, u_hbm, d_hbm, r_hbm, yn, yp,
    out_hbm, ft_hbm, rim,
    ua, ub, dd, rr, kk, fbuf, fin, turned, sems, osem,
):
    cx, cy, _ = u_hbm.shape
    copies = [
        pltpu.make_async_copy(src, dst.at[:, 0:cy], sems.at[i])
        for i, (src, dst) in enumerate(((u_hbm, ua), (d_hbm, dd), (r_hbm, rr)))
    ]
    for copy in copies:
        copy.start()

    def edge_rows(x, carry):
        for which, dst in enumerate((ua, dd, rr)):
            dst[x, cy : cy + W, :] = yn[which, x]
            dst[x, cy + W : cy + 2 * W, :] = yp[which, x]
        return carry

    lax.fori_loop(0, cx, edge_rows, 0)
    work = Plane(dd, rr, kk, fbuf, place)
    for copy in copies:
        copy.wait()

    src, dst = ua, ub
    for step in range(STEPS):
        last = step == STEPS - 1
        low, high = step + 1, cx - 1 - step
        for plane in range(3):
            work.local(src, dst, low - 1 + plane)
        work.face(src, low)

        def body(plane, carry, src=src, dst=dst, last=last, high=high):
            work.across(
                src, dst, fin if last else dst, plane, plane - W if last else plane
            )
            work.local(src, dst, jnp.minimum(plane + 2, high))
            return carry

        lax.fori_loop(low, high, body, 0)
        if not last:
            for i, plane in enumerate((low, low + 1, high - 2, high - 1)):
                rim[4 * step + i] = dst[plane]
            src, dst = dst, src
    done = pltpu.make_async_copy(fin, out_hbm.at[W : cx - W], osem.at[0])
    done.start()
    turn_over(fin.at[8 - W : cx - 8 - W], turned)
    move = pltpu.make_async_copy(turned, ft_hbm, osem.at[1])
    move.start()
    done.wait()
    move.wait()


ANYWHERE = pl.BlockSpec(memory_space=pl.ANY)
LOCAL = pl.BlockSpec(memory_space=pltpu.VMEM)
SCALARS = pl.BlockSpec(memory_space=pltpu.SMEM)


def inner(place, u, d, r, yn, yp):
    cx, cy, nz = u.shape
    wide = pltpu.VMEM((cx, cy + 8, nz), F32)
    return pl.pallas_call(
        inner_kernel,
        out_shape=(
            jax.ShapeDtypeStruct((cx, cy, nz), F32),
            jax.ShapeDtypeStruct((cy, cx - 16, nz), F32),
            jax.ShapeDtypeStruct((4 * (STEPS - 1), cy + 8, nz), F32),
        ),
        in_specs=[SCALARS] + [ANYWHERE] * 3 + [LOCAL] * 2,
        out_specs=(ANYWHERE, ANYWHERE, LOCAL),
        scratch_shapes=[wide] * 5
        + [
            pltpu.VMEM((cy + 8, nz), F32),
            pltpu.VMEM((cx - 2 * W, cy, nz), F32),
            pltpu.VMEM((cy, cx - 16, nz), F32),
            pltpu.SemaphoreType.DMA((3,)),
            pltpu.SemaphoreType.DMA((2,)),
        ],
        cost_estimate=pl.CostEstimate(
            flops=40 * STEPS * cx * cy * nz, bytes_accessed=24 * cx * cy * nz, transcendentals=0
        ),
        name="inner",
    )(place, u, d, r, yn, yp)


SPAN = 2 * W + 1


def outer_kernel(
    place, u_hbm, d_hbm, r_hbm, yn, yp, xm_hbm, xp_hbm, cn, cp, rim, field_hbm,
    out_hbm, ft_hbm,
    ua, ub, dd, rr, kk, fbuf, fin, turned, sems, osem,
):
    cx, cy, nz = u_hbm.shape
    own = slice(0, cy)
    copies = []
    for src, dst in (
        (xm_hbm.at[0:W], ua.at[0:W, own]),
        (u_hbm.at[0:2], ua.at[W : W + 2, own]),
        (u_hbm.at[cx - 2 : cx], ua.at[SPAN + W - 1 : SPAN + W + 1, own]),
        (xp_hbm.at[0:W], ua.at[SPAN + W + 1 : 2 * SPAN, own]),
        (xm_hbm.at[W : 2 * W], dd.at[0:W, own]),
        (d_hbm.at[0 : W + 1], dd.at[W:SPAN, own]),
        (d_hbm.at[cx - W - 1 : cx], dd.at[SPAN : SPAN + W + 1, own]),
        (xp_hbm.at[W : 2 * W], dd.at[SPAN + W + 1 : 2 * SPAN, own]),
        (xm_hbm.at[2 * W : 3 * W - 1], rr.at[1:W, own]),
        (r_hbm.at[0 : W + 1], rr.at[W:SPAN, own]),
        (r_hbm.at[cx - W - 1 : cx], rr.at[SPAN : SPAN + W + 1, own]),
        (xp_hbm.at[2 * W : 3 * W - 1], rr.at[SPAN + W + 1 : 2 * SPAN - 1, own]),
        (field_hbm.at[W:8], fin.at[W:8]),
        (field_hbm.at[cx - 8 : cx - W], fin.at[8 : 16 - W]),
    ):
        copies.append(pltpu.make_async_copy(src, dst, sems.at[len(copies)]))
    for copy in copies:
        copy.start()

    rr[0] = jnp.zeros((cy + 8, nz), F32)
    rr[2 * SPAN - 1] = jnp.zeros((cy + 8, nz), F32)

    def rows(dst, plane, after, before):
        dst[plane, cy : cy + W, :] = after
        dst[plane, cy + W : cy + 2 * W, :] = before

    for i in range(W + 1):
        for base, x in ((W + i, i), (SPAN + i, cx - W - 1 + i)):
            for which, dst in enumerate((ua, dd, rr)):
                rows(dst, base, yn[which, x], yp[which, x])
    for side, base in ((0, 0), (1, SPAN + W + 1)):
        at = side * (3 * W - 1)
        for i in range(W):
            rows(ua, base + i, cn[at + i], cp[at + i])
            rows(dd, base + i, cn[at + W + i], cp[at + W + i])
        for i in range(W - 1):
            rows(rr, base + i + 1 - side, cn[at + 2 * W + i], cp[at + 2 * W + i])
    work = Plane(dd, rr, kk, fbuf, place)
    first = (place[0] > 0).astype(F32)
    final = (place[0] < place[2] - 1).astype(F32)
    for copy in copies:
        copy.wait()

    src, dst = ua, ub
    for step in range(STEPS):
        last = step == STEPS - 1

        def end(side, carry, src=src, dst=dst, step=step, last=last):
            base = jnp.where(side == 0, step, SPAN + W - 1 - step)
            for i in range(3):
                work.local(src, dst, base + i)
            work.face(src, base + 1)
            for j in range(W):
                keep = None
                if not last:
                    keep = jnp.where(
                        side == 0, first if j < W - 1 - step else 1.0, final if j > step else 1.0
                    )
                target = side * (16 - W) + j if last else base + 1 + j
                work.across(src, dst, fin if last else dst, base + 1 + j, target, keep)
                if j < W - 1:
                    work.local(src, dst, base + 3 + j)
            return carry

        lax.fori_loop(0, 2, end, 0)
        if not last:
            for i in range(2):
                dst[step + W + 1 + i] = rim[4 * step + i]
                dst[SPAN + W - 2 - step + i] = rim[4 * step + 2 + i]
            src, dst = dst, src
    done = [
        pltpu.make_async_copy(fin.at[0:W], out_hbm.at[0:W], osem.at[0]),
        pltpu.make_async_copy(fin.at[16 - W : 16], out_hbm.at[cx - W : cx], osem.at[1]),
    ]
    for copy in done:
        copy.start()
    turn_over(fin, turned)
    done.append(pltpu.make_async_copy(turned, ft_hbm, osem.at[2]))
    done[2].start()
    for copy in done:
        copy.wait()


def outer(place, u, d, r, yn, yp, xm, xp, cn, cp, rim, field):
    cx, cy, nz = u.shape
    wide = pltpu.VMEM((2 * SPAN, cy + 8, nz), F32)
    return pl.pallas_call(
        outer_kernel,
        out_shape=(
            jax.ShapeDtypeStruct((cx, cy, nz), F32),
            jax.ShapeDtypeStruct((cy, 16, nz), F32),
        ),
        in_specs=[SCALARS] + [ANYWHERE] * 3 + [LOCAL] * 2 + [ANYWHERE] * 2 + [LOCAL] * 3 + [ANYWHERE],
        out_specs=(ANYWHERE, ANYWHERE),
        scratch_shapes=[wide] * 5
        + [
            pltpu.VMEM((cy + 8, nz), F32),
            pltpu.VMEM((16, cy, nz), F32),
            pltpu.VMEM((cy, 16, nz), F32),
            pltpu.SemaphoreType.DMA((14,)),
            pltpu.SemaphoreType.DMA((3,)),
        ],
        input_output_aliases={11: 0},
        name="outer",
    )(place, u, d, r, yn, yp, xm, xp, cn, cp, rim, field)


def render_kernel(whole, part, cen, lev, mix, ft, sign_ref, *rest):
    out, moved = rest[-2:]
    view = pl.program_id(1)
    depth, rows, nz = ft.shape
    blocks = nz // 128
    zero = jnp.zeros((rows, 128), F32)

    @pl.when(view == 0)
    def _():
        lane = lax.broadcasted_iota(jnp.int32, (rows, 128), 1)

        def shifts(y, carry):
            cells = [ft[y, :, 128 * b : 128 * b + 128] for b in range(blocks)]
            for b in range(blocks):
                moved[y, 0, :, 128 * b : 128 * b + 128] = cells[b]
            for n in range(1, MAXSHIFT + 1):
                back = [pltpu.roll(c, 128 - n, 1) for c in cells] + [zero]
                keep = lane < 128 - n
                for b in range(blocks):
                    moved[y, n, :, 128 * b : 128 * b + 128] = jnp.where(keep, back[b], back[b + 1])
            return carry

        lax.fori_loop(0, depth, shifts, 0, unroll=2)

    for b in range(blocks):
        at = slice(128 * b, 128 * b + 128)
        sign = jnp.broadcast_to(sign_ref[0, :, at], (rows, 128))
        rising = sign < 0.0
        light = jnp.ones((rows, 128), F32)
        sums = [zero] * BUMPS
        for y in range(depth):
            n = whole[view, y]
            near = moved[y, n, :, at]
            s = near + part[view, y] * (moved[y, n + 1, :, at] - near)
            bumps = []
            for i in range(BUMPS):
                t = s - cen[i]
                bumps.append(jnp.exp2(lev[i] - t * t))
            pairs = [bumps[i] + bumps[i + 1] for i in range(0, BUMPS, 2)]
            total = (pairs[0] + pairs[1]) + (pairs[2] + pairs[3])
            after = light * jnp.exp2(total * sign)
            weight = light - after
            light = after
            sums = [sums[i] + bumps[i] * weight for i in range(BUMPS)]
        inverse = 1.0 / light
        through = jnp.where(rising, light, inverse)
        scale = jnp.where(rising, 1.0, -inverse)
        channels = []
        for c in range(3):
            value = mix[c, 0] * sums[0]
            for i in range(1, BUMPS):
                value = value + mix[c, i] * sums[i]
            channels.append(value * scale)
        channels.append(through)
        for d in range(rows // 2):
            out[d, :, at] = jnp.concatenate([c[2 * d : 2 * d + 2] for c in channels], axis=0)


def render(whole, part, cen, lev, mix, ft, signs, spread, count, parts=None):
    cy, cx, nz = ft.shape
    operands = [whole, part, cen, lev, mix, ft, signs]
    in_specs = [SCALARS] * 5 + [
        pl.BlockSpec((cy, 8, nz), lambda i, v: (0, i, 0)),
        pl.BlockSpec((1, 1, nz), lambda i, v: (v, 0, 0)),
    ]
    aliases = {}
    if parts is not None:
        operands.append(parts)
        in_specs.append(ANYWHERE)
        aliases = {7: 0}
    cells = VIEWS * cx * cy * nz
    return pl.pallas_call(
        render_kernel,
        out_shape=jax.ShapeDtypeStruct((count, 8 * VIEWS, nz), F32),
        grid=(cx // 8, VIEWS),
        in_specs=in_specs,
        out_specs=pl.BlockSpec((4, 8, nz), lambda i, v: (spread(i), v, 0)),
        scratch_shapes=[pltpu.VMEM((cy, MAXSHIFT + 1, 8, nz), F32)],
        input_output_aliases=aliases,
        cost_estimate=pl.CostEstimate(
            flops=60 * cells, bytes_accessed=4 * (cx * cy + count * 8 * VIEWS) * nz, transcendentals=9 * cells
        ),
        name="render",
    )(*operands)


def combine_kernel(parts, sign_ref, image, trans):
    count, _, nz = parts.shape
    sub = lax.broadcasted_iota(jnp.int32, (8, nz), 0)
    for view in range(VIEWS):
        rising = jnp.broadcast_to(sign_ref[view], (8, nz)) < 0.0
        total = jnp.zeros((8, nz), F32)
        ahead = jnp.ones((8, nz), F32)
        for source in range(count):
            block = parts[source, 8 * view : 8 * view + 8, :]
            tail = jnp.where(sub >= 6, block, 0.0)
            pair = tail + pltpu.roll(tail, 4, 0)
            light = pair + pltpu.roll(pair, 2, 0)
            total = total * jnp.where(rising, 1.0, light) + block * jnp.where(rising, ahead, 1.0)
            ahead = ahead * light
        for c in range(3):
            image[view, c] = total[2 * c : 2 * c + 2]
        trans[view] = ahead[6:8]


def combine(parts, signs):
    nz = parts.shape[2]
    return pl.pallas_call(
        combine_kernel,
        out_shape=(
            jax.ShapeDtypeStruct((VIEWS, 3, 2, nz), F32),
            jax.ShapeDtypeStruct((VIEWS, 2, nz), F32),
        ),
        name="combine",
    )(parts, signs)


def scene_of(u, d, r, offsets, depth_order, centres, colour, opacity):
    cx, cy, _ = u.shape
    place = jnp.stack(
        [
            lax.axis_index("sx"),
            lax.axis_index("sy"),
            jnp.int32(lax.axis_size("sx")),
            jnp.int32(lax.axis_size("sy")),
        ]
    ).astype(jnp.int32)
    up_x = jnp.concatenate([u[cx - W :], d[cx - W :], r[cx - W + 1 :]])
    down_x = jnp.concatenate([u[:W], d[:W], r[: W - 1]])
    xm = shift(up_x, "sx", True)
    xp = shift(down_x, "sx", False)
    up_y = jnp.stack([a[:, cy - W :] for a in (u, d, r)])
    down_y = jnp.stack([a[:, :W] for a in (u, d, r)])
    yp = shift(up_y, "sy", True)
    yn = shift(down_y, "sy", False)
    cp = shift(jnp.concatenate([xm[:, cy - W :], xp[:, cy - W :]]), "sy", True)
    cn = shift(jnp.concatenate([xm[:, :W], xp[:, :W]]), "sy", False)
    offs = lax.dynamic_slice_in_dim(offsets, lax.axis_index("sy") * cy, cy, 1)
    signs = jnp.where(depth_order == 0, -1.0, 1.0).astype(F32)[:, None, :]
    level = opacity * LOG2E
    scene = (offs // 4, (offs % 4).astype(F32) * 0.25, centres * GAIN, jnp.log2(level), colour / level)

    field, turned, rim = inner(place, u, d, r, yn, yp)
    parts = render(*scene, turned, signs, lambda i: i + 1, cx // 2)
    field, turned = outer(place, u, d, r, yn, yp, xm, xp, cn, cp, rim, field)
    parts = render(*scene, turned, signs, lambda i: 3 * i, cx // 2, parts)
    parts = lax.all_to_all(parts, "sy", split_axis=0, concat_axis=0, tiled=True)
    image, trans = combine(parts, signs)
    return field, image, trans


def solution(mesh):
    grid = P("sx", "sy", None)
    return jax.shard_map(
        scene_of,
        mesh=mesh,
        in_specs=(grid, grid, grid, P(), P(), P(), P(), P()),
        out_specs=(
            grid,
            P(None, None, ("sx", "sy"), None),
            P(None, ("sx", "sy"), None),
        ),
        check_vma=False,
    )
```

```python
import jax
import jax.numpy as jnp
from jax import lax
from jax.experimental import pallas as pl
from jax.experimental.pallas import tpu as pltpu
from jax.sharding import PartitionSpec as P


STEPS = 4
VIEWS = 4
BUMPS = 8
W = STEPS
LOG2E = 1.4426950408889634
GAIN = 2.0 * LOG2E**0.5

F32 = jnp.float32


def shift(value, axis, up):
    size = lax.axis_size(axis)
    pairs = [(i, i + 1) for i in range(size - 1)]
    if not up:
        pairs = [(j, i) for i, j in pairs]
    return lax.ppermute(value, axis, pairs)


def cut(tile, block):
    return (slice(8 * tile, 8 * tile + 8), slice(128 * block, 128 * block + 128))


class Plane:
    def __init__(self, dd, rr, kk, fbuf, place):
        self.dd, self.rr, self.kk, self.fbuf = dd, rr, kk, fbuf
        self.tiles, self.blocks = dd.shape[1] // 8, dd.shape[2] // 128
        sub = lax.broadcasted_iota(jnp.int32, (8, 128), 0)
        lane = lax.broadcasted_iota(jnp.int32, (8, 128), 1)
        self.sub_last, self.sub_first = sub == 7, sub == 0
        self.lane_last, self.lane_first = lane == 127, lane == 0
        self.zero = jnp.zeros((8, 128), F32)
        self.inside = jnp.where(
            sub < W, (place[1] < place[3] - 1).astype(F32), (place[1] > 0).astype(F32)
        )

    def local(self, src, dst, plane):
        blocks = self.blocks
        for t in range(self.tiles):
            u = [src[(plane,) + cut(t, b)] for b in range(blocks)]
            warm = [jnp.tanh(v) for v in u]
            k = [self.dd[(plane,) + cut(t, b)] * (0.5 + 0.2 * warm[b]) for b in range(blocks)]
            u_up = [pltpu.roll(v, 127, 1) for v in u] + [self.zero]
            k_up = [pltpu.roll(v, 127, 1) for v in k] + [self.zero]
            flux = []
            for b in range(blocks):
                un = jnp.where(self.lane_last, u_up[b + 1], u_up[b])
                kn = jnp.where(self.lane_last, k_up[b + 1], k_up[b])
                flux.append((k[b] + kn) * (un - u[b]))
            down = [pltpu.roll(v, 1, 1) for v in flux]
            for b in range(blocks):
                at = (plane,) + cut(t, b)
                low = jnp.where(self.lane_first, k[b] * u[b] if b == 0 else down[b - 1], down[b])
                self.kk[at] = k[b]
                dst[at] = u[b] + ((flux[b] - low) + self.rr[at] * warm[b])

    def face(self, src, plane):
        for t in range(self.tiles):
            for b in range(self.blocks):
                at = cut(t, b)
                self.fbuf[at] = (self.kk[(plane - 1,) + at] + self.kk[(plane,) + at]) * (
                    src[(plane,) + at] - src[(plane - 1,) + at]
                )

    def across(self, src, base, dst, plane, target, keep=None):
        tiles, kk = self.tiles, self.kk
        for b in range(self.blocks):
            u = [src[(plane,) + cut(t, b)] for t in range(tiles)]
            k = [kk[(plane,) + cut(t, b)] for t in range(tiles)]
            u_up = [pltpu.roll(v, 7, 0) for v in u]
            k_up = [pltpu.roll(v, 7, 0) for v in k]
            flux = []
            for t in range(tiles):
                n = (t + 1) % tiles
                un = jnp.where(self.sub_last, u_up[n], u_up[t])
                kn = jnp.where(self.sub_last, k_up[n], k_up[t])
                flux.append((k[t] + kn) * (un - u[t]))
            down = [pltpu.roll(v, 1, 0) for v in flux]
            for t in range(min(tiles, dst.shape[1] // 8)):
                at = cut(t, b)
                change = flux[t] - jnp.where(self.sub_first, down[t - 1], down[t])
                fx = (k[t] + kk[(plane + 1,) + at]) * (src[(plane + 1,) + at] - u[t])
                new = base[(plane,) + at] + (change + (fx - self.fbuf[at]))
                self.fbuf[at] = fx
                if t == tiles - 1:
                    new = new * self.inside
                if keep is not None:
                    new = new * keep
                dst[(target,) + at] = new


def turn_over(field, turned):
    cx, cy, nz = field.shape[0], field.shape[1], field.shape[2]

    def group(xg, carry):
        rows = pl.ds(pl.multiple_of(8 * xg, 8), 8)
        for yg in range(cy // 8):
            for b in range(nz // 128):
                columns = slice(128 * b, 128 * b + 128)
                piece = field[rows, 8 * yg : 8 * yg + 8, columns]
                turned[8 * yg : 8 * yg + 8, rows, columns] = jnp.transpose(piece, (1, 0, 2)) * GAIN
        return carry

    lax.fori_loop(0, cx // 8, group, 0)


def inner_kernel(
    place, u_hbm, d_hbm, r_hbm, yn, yp,
    out_hbm, ft_hbm, rim,
    ua, ub, dd, rr, kk, fbuf, fin, turned, sems, osem,
):
    cx, cy, _ = u_hbm.shape
    copies = [
        pltpu.make_async_copy(src, dst.at[:, 0:cy], sems.at[i])
        for i, (src, dst) in enumerate(((u_hbm, ua), (d_hbm, dd), (r_hbm, rr)))
    ]
    for copy in copies:
        copy.start()

    def edge_rows(x, carry):
        for which, dst in enumerate((ua, dd, rr)):
            dst[x, cy : cy + W, :] = yn[which, x]
            dst[x, cy + W : cy + 2 * W, :] = yp[which, x]
        return carry

    lax.fori_loop(0, cx, edge_rows, 0)
    work = Plane(dd, rr, kk, fbuf, place)
    for copy in copies:
        copy.wait()

    src, dst = ua, ub
    for step in range(STEPS):
        last = step == STEPS - 1
        low, high = step + 1, cx - 1 - step
        for plane in range(3):
            work.local(src, dst, low - 1 + plane)
        work.face(src, low)

        def body(plane, carry, src=src, dst=dst, last=last, high=high):
            work.across(
                src, dst, fin if last else dst, plane, plane - W if last else plane
            )
            work.local(src, dst, jnp.minimum(plane + 2, high))
            return carry

        lax.fori_loop(low, high, body, 0)
        if not last:
            for i, plane in enumerate((low, low + 1, high - 2, high - 1)):
                rim[4 * step + i] = dst[plane]
            src, dst = dst, src
    done = pltpu.make_async_copy(fin, out_hbm.at[W : cx - W], osem.at[0])
    done.start()
    turn_over(fin.at[8 - W : cx - 8 - W], turned)
    move = pltpu.make_async_copy(turned, ft_hbm, osem.at[1])
    move.start()
    done.wait()
    move.wait()


ANYWHERE = pl.BlockSpec(memory_space=pl.ANY)
LOCAL = pl.BlockSpec(memory_space=pltpu.VMEM)
SCALARS = pl.BlockSpec(memory_space=pltpu.SMEM)


def inner(place, u, d, r, yn, yp):
    cx, cy, nz = u.shape
    wide = pltpu.VMEM((cx, cy + 8, nz), F32)
    return pl.pallas_call(
        inner_kernel,
        out_shape=(
            jax.ShapeDtypeStruct((cx, cy, nz), F32),
            jax.ShapeDtypeStruct((cy, cx - 16, nz), F32),
            jax.ShapeDtypeStruct((4 * (STEPS - 1), cy + 8, nz), F32),
        ),
        in_specs=[SCALARS] + [ANYWHERE] * 3 + [LOCAL] * 2,
        out_specs=(ANYWHERE, ANYWHERE, LOCAL),
        scratch_shapes=[wide] * 5
        + [
            pltpu.VMEM((cy + 8, nz), F32),
            pltpu.VMEM((cx - 2 * W, cy, nz), F32),
            pltpu.VMEM((cy, cx - 16, nz), F32),
            pltpu.SemaphoreType.DMA((3,)),
            pltpu.SemaphoreType.DMA((2,)),
        ],
        cost_estimate=pl.CostEstimate(
            flops=40 * STEPS * cx * cy * nz, bytes_accessed=24 * cx * cy * nz, transcendentals=0
        ),
        name="inner",
    )(place, u, d, r, yn, yp)


SPAN = 2 * W + 1


def outer_kernel(
    place, u_hbm, d_hbm, r_hbm, yn, yp, xm_hbm, xp_hbm, cn, cp, rim, field_hbm,
    out_hbm, ft_hbm,
    ua, ub, dd, rr, kk, fbuf, fin, turned, sems, osem,
):
    cx, cy, nz = u_hbm.shape
    own = slice(0, cy)
    copies = []
    for src, dst in (
        (xm_hbm.at[0:W], ua.at[0:W, own]),
        (u_hbm.at[0:2], ua.at[W : W + 2, own]),
        (u_hbm.at[cx - 2 : cx], ua.at[SPAN + W - 1 : SPAN + W + 1, own]),
        (xp_hbm.at[0:W], ua.at[SPAN + W + 1 : 2 * SPAN, own]),
        (xm_hbm.at[W : 2 * W], dd.at[0:W, own]),
        (d_hbm.at[0 : W + 1], dd.at[W:SPAN, own]),
        (d_hbm.at[cx - W - 1 : cx], dd.at[SPAN : SPAN + W + 1, own]),
        (xp_hbm.at[W : 2 * W], dd.at[SPAN + W + 1 : 2 * SPAN, own]),
        (xm_hbm.at[2 * W : 3 * W - 1], rr.at[1:W, own]),
        (r_hbm.at[0 : W + 1], rr.at[W:SPAN, own]),
        (r_hbm.at[cx - W - 1 : cx], rr.at[SPAN : SPAN + W + 1, own]),
        (xp_hbm.at[2 * W : 3 * W - 1], rr.at[SPAN + W + 1 : 2 * SPAN - 1, own]),
        (field_hbm.at[W:8], fin.at[W:8]),
        (field_hbm.at[cx - 8 : cx - W], fin.at[8 : 16 - W]),
    ):
        copies.append(pltpu.make_async_copy(src, dst, sems.at[len(copies)]))
    for copy in copies:
        copy.start()

    rr[0] = jnp.zeros((cy + 8, nz), F32)
    rr[2 * SPAN - 1] = jnp.zeros((cy + 8, nz), F32)

    def rows(dst, plane, after, before):
        dst[plane, cy : cy + W, :] = after
        dst[plane, cy + W : cy + 2 * W, :] = before

    for i in range(W + 1):
        for base, x in ((W + i, i), (SPAN + i, cx - W - 1 + i)):
            for which, dst in enumerate((ua, dd, rr)):
                rows(dst, base, yn[which, x], yp[which, x])
    for side, base in ((0, 0), (1, SPAN + W + 1)):
        at = side * (3 * W - 1)
        for i in range(W):
            rows(ua, base + i, cn[at + i], cp[at + i])
            rows(dd, base + i, cn[at + W + i], cp[at + W + i])
        for i in range(W - 1):
            rows(rr, base + i + 1 - side, cn[at + 2 * W + i], cp[at + 2 * W + i])
    work = Plane(dd, rr, kk, fbuf, place)
    first = (place[0] > 0).astype(F32)
    final = (place[0] < place[2] - 1).astype(F32)
    for copy in copies:
        copy.wait()

    src, dst = ua, ub
    for step in range(STEPS):
        last = step == STEPS - 1

        def end(side, carry, src=src, dst=dst, step=step, last=last):
            base = jnp.where(side == 0, step, SPAN + W - 1 - step)
            for i in range(3):
                work.local(src, dst, base + i)
            work.face(src, base + 1)
            for j in range(W):
                keep = None
                if not last:
                    keep = jnp.where(
                        side == 0, first if j < W - 1 - step else 1.0, final if j > step else 1.0
                    )
                target = side * (16 - W) + j if last else base + 1 + j
                work.across(src, dst, fin if last else dst, base + 1 + j, target, keep)
                if j < W - 1:
                    work.local(src, dst, base + 3 + j)
            return carry

        lax.fori_loop(0, 2, end, 0)
        if not last:
            for i in range(2):
                dst[step + W + 1 + i] = rim[4 * step + i]
                dst[SPAN + W - 2 - step + i] = rim[4 * step + 2 + i]
            src, dst = dst, src
    done = [
        pltpu.make_async_copy(fin.at[0:W], out_hbm.at[0:W], osem.at[0]),
        pltpu.make_async_copy(fin.at[16 - W : 16], out_hbm.at[cx - W : cx], osem.at[1]),
    ]
    for copy in done:
        copy.start()
    turn_over(fin, turned)
    done.append(pltpu.make_async_copy(turned, ft_hbm, osem.at[2]))
    done[2].start()
    for copy in done:
        copy.wait()


def outer(place, u, d, r, yn, yp, xm, xp, cn, cp, rim, field):
    cx, cy, nz = u.shape
    wide = pltpu.VMEM((2 * SPAN, cy + 8, nz), F32)
    return pl.pallas_call(
        outer_kernel,
        out_shape=(
            jax.ShapeDtypeStruct((cx, cy, nz), F32),
            jax.ShapeDtypeStruct((cy, 16, nz), F32),
        ),
        in_specs=[SCALARS] + [ANYWHERE] * 3 + [LOCAL] * 2 + [ANYWHERE] * 2 + [LOCAL] * 3 + [ANYWHERE],
        out_specs=(ANYWHERE, ANYWHERE),
        scratch_shapes=[wide] * 5
        + [
            pltpu.VMEM((cy + 8, nz), F32),
            pltpu.VMEM((16, cy, nz), F32),
            pltpu.VMEM((cy, 16, nz), F32),
            pltpu.SemaphoreType.DMA((14,)),
            pltpu.SemaphoreType.DMA((3,)),
        ],
        input_output_aliases={11: 0},
        name="outer",
    )(place, u, d, r, yn, yp, xm, xp, cn, cp, rim, field)


def render_kernel(whole, part, cen, lev, mix, ft, sign_ref, *rest):
    out, moved = rest[-2:]
    view = pl.program_id(1)
    depth, rows, nz = ft.shape
    blocks = nz // 128
    zero = jnp.zeros((rows, 128), F32)

    @pl.when(view == 0)
    def _():
        lane = lax.broadcasted_iota(jnp.int32, (rows, 128), 1)
        lane_last = lane == 127

        def shear(y, carry):
            cells = [ft[y, :, 128 * b : 128 * b + 128] for b in range(blocks)]
            back = [pltpu.roll(c, 127, 1) for c in cells] + [zero]
            slope = [jnp.where(lane_last, back[b + 1], back[b]) - cells[b] for b in range(blocks)]
            for v in range(VIEWS):
                n, f = whole[v, y], part[v, y]
                turn = lax.rem(128 - n, 128)
                keep = lane < 128 - n
                back = [pltpu.roll(cells[b] + f * slope[b], turn, 1) for b in range(blocks)] + [zero]
                for b in range(blocks):
                    moved[v, y, :, 128 * b : 128 * b + 128] = jnp.where(keep, back[b], back[b + 1])
            return carry

        lax.fori_loop(0, depth, shear, 0, unroll=8)

    for b in range(blocks):
        at = slice(128 * b, 128 * b + 128)
        sign = jnp.broadcast_to(sign_ref[0, :, at], (rows, 128))
        rising = sign < 0.0
        light = jnp.ones((rows, 128), F32)
        sums = [zero] * BUMPS
        for y in range(depth):
            s = moved[view, y, :, at]
            bumps = []
            for i in range(BUMPS):
                t = s - cen[i]
                bumps.append(jnp.exp2(lev[i] - t * t))
            pairs = [bumps[i] + bumps[i + 1] for i in range(0, BUMPS, 2)]
            total = (pairs[0] + pairs[1]) + (pairs[2] + pairs[3])
            after = light * jnp.exp2(total * sign)
            weight = light - after
            light = after
            sums = [sums[i] + bumps[i] * weight for i in range(BUMPS)]
        inverse = 1.0 / light
        through = jnp.where(rising, light, inverse)
        scale = jnp.where(rising, 1.0, -inverse)
        channels = []
        for c in range(3):
            value = mix[c, 0] * sums[0]
            for i in range(1, BUMPS):
                value = value + mix[c, i] * sums[i]
            channels.append(value * scale)
        channels.append(through)
        for d in range(rows // 2):
            out[d, :, at] = jnp.concatenate([c[2 * d : 2 * d + 2] for c in channels], axis=0)


def render(whole, part, cen, lev, mix, ft, signs, spread, count, parts=None):
    cy, cx, nz = ft.shape
    operands = [whole, part, cen, lev, mix, ft, signs]
    in_specs = [SCALARS] * 5 + [
        pl.BlockSpec((cy, 8, nz), lambda i, v: (0, i, 0)),
        pl.BlockSpec((1, 1, nz), lambda i, v: (v, 0, 0)),
    ]
    aliases = {}
    if parts is not None:
        operands.append(parts)
        in_specs.append(ANYWHERE)
        aliases = {7: 0}
    cells = VIEWS * cx * cy * nz
    return pl.pallas_call(
        render_kernel,
        out_shape=jax.ShapeDtypeStruct((count, 8 * VIEWS, nz), F32),
        grid=(cx // 8, VIEWS),
        in_specs=in_specs,
        out_specs=pl.BlockSpec((4, 8, nz), lambda i, v: (spread(i), v, 0)),
        scratch_shapes=[pltpu.VMEM((VIEWS, cy, 8, nz), F32)],
        input_output_aliases=aliases,
        cost_estimate=pl.CostEstimate(
            flops=60 * cells, bytes_accessed=4 * (cx * cy + count * 8 * VIEWS) * nz, transcendentals=9 * cells
        ),
        name="render",
    )(*operands)


def combine_kernel(parts, sign_ref, image, trans):
    count, _, nz = parts.shape
    sub = lax.broadcasted_iota(jnp.int32, (8, nz), 0)
    for view in range(VIEWS):
        rising = jnp.broadcast_to(sign_ref[view], (8, nz)) < 0.0
        total = jnp.zeros((8, nz), F32)
        ahead = jnp.ones((8, nz), F32)
        for source in range(count):
            block = parts[source, 8 * view : 8 * view + 8, :]
            tail = jnp.where(sub >= 6, block, 0.0)
            pair = tail + pltpu.roll(tail, 4, 0)
            light = pair + pltpu.roll(pair, 2, 0)
            total = total * jnp.where(rising, 1.0, light) + block * jnp.where(rising, ahead, 1.0)
            ahead = ahead * light
        for c in range(3):
            image[view, c] = total[2 * c : 2 * c + 2]
        trans[view] = ahead[6:8]


def combine(parts, signs):
    nz = parts.shape[2]
    return pl.pallas_call(
        combine_kernel,
        out_shape=(
            jax.ShapeDtypeStruct((VIEWS, 3, 2, nz), F32),
            jax.ShapeDtypeStruct((VIEWS, 2, nz), F32),
        ),
        name="combine",
    )(parts, signs)


def scene_of(u, d, r, offsets, depth_order, centres, colour, opacity):
    cx, cy, _ = u.shape
    place = jnp.stack(
        [
            lax.axis_index("sx"),
            lax.axis_index("sy"),
            jnp.int32(lax.axis_size("sx")),
            jnp.int32(lax.axis_size("sy")),
        ]
    ).astype(jnp.int32)
    up_x = jnp.concatenate([u[cx - W :], d[cx - W :], r[cx - W + 1 :]])
    down_x = jnp.concatenate([u[:W], d[:W], r[: W - 1]])
    xm = shift(up_x, "sx", True)
    xp = shift(down_x, "sx", False)
    up_y = jnp.stack([a[:, cy - W :] for a in (u, d, r)])
    down_y = jnp.stack([a[:, :W] for a in (u, d, r)])
    yp = shift(up_y, "sy", True)
    yn = shift(down_y, "sy", False)
    cp = shift(jnp.concatenate([xm[:, cy - W :], xp[:, cy - W :]]), "sy", True)
    cn = shift(jnp.concatenate([xm[:, :W], xp[:, :W]]), "sy", False)
    offs = lax.dynamic_slice_in_dim(offsets, lax.axis_index("sy") * cy, cy, 1)
    signs = jnp.where(depth_order == 0, -1.0, 1.0).astype(F32)[:, None, :]
    level = opacity * LOG2E
    scene = (offs // 4, (offs % 4).astype(F32) * 0.25, centres * GAIN, jnp.log2(level), colour / level)

    field, turned, rim = inner(place, u, d, r, yn, yp)
    parts = render(*scene, turned, signs, lambda i: i + 1, cx // 2)
    field, turned = outer(place, u, d, r, yn, yp, xm, xp, cn, cp, rim, field)
    parts = render(*scene, turned, signs, lambda i: 3 * i, cx // 2, parts)
    parts = lax.all_to_all(parts, "sy", split_axis=0, concat_axis=0, tiled=True)
    image, trans = combine(parts, signs)
    return field, image, trans


def solution(mesh):
    grid = P("sx", "sy", None)
    return jax.shard_map(
        scene_of,
        mesh=mesh,
        in_specs=(grid, grid, grid, P(), P(), P(), P(), P()),
        out_specs=(
            grid,
            P(None, None, ("sx", "sy"), None),
            P(None, ("sx", "sy"), None),
        ),
        check_vma=False,
    )
```

```python
import jax
import jax.numpy as jnp
from jax import lax
from jax.experimental import pallas as pl
from jax.experimental.pallas import tpu as pltpu
from jax.sharding import PartitionSpec as P


STEPS = 4
VIEWS = 4
BUMPS = 8
W = STEPS
LOG2E = 1.4426950408889634
GAIN = 2.0 * LOG2E**0.5

F32 = jnp.float32


def shift(value, axis, up):
    size = lax.axis_size(axis)
    pairs = [(i, i + 1) for i in range(size - 1)]
    if not up:
        pairs = [(j, i) for i, j in pairs]
    return lax.ppermute(value, axis, pairs)


def cut(tile, block):
    return (slice(8 * tile, 8 * tile + 8), slice(128 * block, 128 * block + 128))


class Plane:
    def __init__(self, dd, dn, rr, kk, fbuf, place):
        self.dd, self.dn, self.rr, self.kk, self.fbuf = dd, dn, rr, kk, fbuf
        self.tiles, self.blocks = dd.shape[1] // 8, dd.shape[2] // 128
        sub = lax.broadcasted_iota(jnp.int32, (8, 128), 0)
        lane = lax.broadcasted_iota(jnp.int32, (8, 128), 1)
        self.sub_last, self.sub_first = sub == 7, sub == 0
        self.lane_last, self.lane_first = lane == 127, lane == 0
        self.zero = jnp.zeros((8, 128), F32)
        self.inside = jnp.where(
            sub < W, (place[1] < place[3] - 1).astype(F32), (place[1] > 0).astype(F32)
        )

    def prepare(self, plane):
        for t in range(self.tiles):
            up = [pltpu.roll(self.dd[(plane,) + cut(t, b)], 127, 1) for b in range(self.blocks)]
            up.append(self.zero)
            for b in range(self.blocks):
                self.dn[(plane,) + cut(t, b)] = jnp.where(self.lane_last, up[b + 1], up[b])

    def local(self, src, dst, plane):
        blocks = self.blocks
        for t in range(self.tiles):
            u = [src[(plane,) + cut(t, b)] for b in range(blocks)]
            warm = [jnp.tanh(v) for v in u]
            k = [self.dd[(plane,) + cut(t, b)] * (0.5 + 0.2 * warm[b]) for b in range(blocks)]
            u_up = [pltpu.roll(v, 127, 1) for v in u] + [self.zero]
            flux = []
            for b in range(blocks):
                un = jnp.where(self.lane_last, u_up[b + 1], u_up[b])
                kn = self.dn[(plane,) + cut(t, b)] * (0.5 + 0.2 * jnp.tanh(un))
                flux.append((k[b] + kn) * (un - u[b]))
            down = [pltpu.roll(v, 1, 1) for v in flux]
            for b in range(blocks):
                at = (plane,) + cut(t, b)
                low = jnp.where(self.lane_first, k[b] * u[b] if b == 0 else down[b - 1], down[b])
                self.kk[at] = k[b]
                dst[at] = u[b] + ((flux[b] - low) + self.rr[at] * warm[b])

    def face(self, src, plane):
        for t in range(self.tiles):
            for b in range(self.blocks):
                at = cut(t, b)
                self.fbuf[at] = (self.kk[(plane - 1,) + at] + self.kk[(plane,) + at]) * (
                    src[(plane,) + at] - src[(plane - 1,) + at]
                )

    def across(self, src, base, dst, plane, target, keep=None):
        tiles, kk = self.tiles, self.kk
        for b in range(self.blocks):
            u = [src[(plane,) + cut(t, b)] for t in range(tiles)]
            k = [kk[(plane,) + cut(t, b)] for t in range(tiles)]
            u_up = [pltpu.roll(v, 7, 0) for v in u]
            k_up = [pltpu.roll(v, 7, 0) for v in k]
            flux = []
            for t in range(tiles):
                n = (t + 1) % tiles
                un = jnp.where(self.sub_last, u_up[n], u_up[t])
                kn = jnp.where(self.sub_last, k_up[n], k_up[t])
                flux.append((k[t] + kn) * (un - u[t]))
            down = [pltpu.roll(v, 1, 0) for v in flux]
            for t in range(min(tiles, dst.shape[1] // 8)):
                at = cut(t, b)
                change = flux[t] - jnp.where(self.sub_first, down[t - 1], down[t])
                fx = (k[t] + kk[(plane + 1,) + at]) * (src[(plane + 1,) + at] - u[t])
                new = base[(plane,) + at] + (change + (fx - self.fbuf[at]))
                self.fbuf[at] = fx
                if t == tiles - 1:
                    new = new * self.inside
                if keep is not None:
                    new = new * keep
                dst[(target,) + at] = new


def turn_over(field, turned):
    cx, cy, nz = field.shape[0], field.shape[1], field.shape[2]

    def group(xg, carry):
        rows = pl.ds(pl.multiple_of(8 * xg, 8), 8)
        for yg in range(cy // 8):
            for b in range(nz // 128):
                columns = slice(128 * b, 128 * b + 128)
                piece = field[rows, 8 * yg : 8 * yg + 8, columns]
                turned[8 * yg : 8 * yg + 8, rows, columns] = jnp.transpose(piece, (1, 0, 2)) * GAIN
        return carry

    lax.fori_loop(0, cx // 8, group, 0)


def inner_kernel(
    place, u_hbm, d_hbm, r_hbm, yn, yp,
    out_hbm, ft_hbm, rim,
    ua, ub, dd, dn, rr, kk, fbuf, fin, turned, sems, osem,
):
    cx, cy, _ = u_hbm.shape
    copies = [
        pltpu.make_async_copy(src, dst.at[:, 0:cy], sems.at[i])
        for i, (src, dst) in enumerate(((u_hbm, ua), (d_hbm, dd), (r_hbm, rr)))
    ]
    for copy in copies:
        copy.start()

    def edge_rows(x, carry):
        for which, dst in enumerate((ua, dd, rr)):
            dst[x, cy : cy + W, :] = yn[which, x]
            dst[x, cy + W : cy + 2 * W, :] = yp[which, x]
        return carry

    lax.fori_loop(0, cx, edge_rows, 0)
    work = Plane(dd, dn, rr, kk, fbuf, place)
    for copy in copies:
        copy.wait()
    lax.fori_loop(0, dd.shape[0], lambda i, c: (work.prepare(i), c)[1], 0, unroll=2)

    src, dst = ua, ub
    for step in range(STEPS):
        last = step == STEPS - 1
        low, high = step + 1, cx - 1 - step
        for plane in range(3):
            work.local(src, dst, low - 1 + plane)
        work.face(src, low)

        def body(plane, carry, src=src, dst=dst, last=last, high=high):
            work.across(
                src, dst, fin if last else dst, plane, plane - W if last else plane
            )
            work.local(src, dst, jnp.minimum(plane + 2, high))
            return carry

        lax.fori_loop(low, high, body, 0)
        if not last:
            for i, plane in enumerate((low, low + 1, high - 2, high - 1)):
                rim[4 * step + i] = dst[plane]
            src, dst = dst, src
    done = pltpu.make_async_copy(fin, out_hbm.at[W : cx - W], osem.at[0])
    done.start()
    turn_over(fin.at[8 - W : cx - 8 - W], turned)
    move = pltpu.make_async_copy(turned, ft_hbm, osem.at[1])
    move.start()
    done.wait()
    move.wait()


ANYWHERE = pl.BlockSpec(memory_space=pl.ANY)
LOCAL = pl.BlockSpec(memory_space=pltpu.VMEM)
SCALARS = pl.BlockSpec(memory_space=pltpu.SMEM)


def inner(place, u, d, r, yn, yp):
    cx, cy, nz = u.shape
    wide = pltpu.VMEM((cx, cy + 8, nz), F32)
    return pl.pallas_call(
        inner_kernel,
        out_shape=(
            jax.ShapeDtypeStruct((cx, cy, nz), F32),
            jax.ShapeDtypeStruct((cy, cx - 16, nz), F32),
            jax.ShapeDtypeStruct((4 * (STEPS - 1), cy + 8, nz), F32),
        ),
        in_specs=[SCALARS] + [ANYWHERE] * 3 + [LOCAL] * 2,
        out_specs=(ANYWHERE, ANYWHERE, LOCAL),
        scratch_shapes=[wide] * 6
        + [
            pltpu.VMEM((cy + 8, nz), F32),
            pltpu.VMEM((cx - 2 * W, cy, nz), F32),
            pltpu.VMEM((cy, cx - 16, nz), F32),
            pltpu.SemaphoreType.DMA((3,)),
            pltpu.SemaphoreType.DMA((2,)),
        ],
        cost_estimate=pl.CostEstimate(
            flops=40 * STEPS * cx * cy * nz, bytes_accessed=24 * cx * cy * nz, transcendentals=0
        ),
        name="inner",
    )(place, u, d, r, yn, yp)


SPAN = 2 * W + 1


def outer_kernel(
    place, u_hbm, d_hbm, r_hbm, yn, yp, xm_hbm, xp_hbm, cn, cp, rim, field_hbm,
    out_hbm, ft_hbm,
    ua, ub, dd, dn, rr, kk, fbuf, fin, turned, sems, osem,
):
    cx, cy, nz = u_hbm.shape
    own = slice(0, cy)
    copies = []
    for src, dst in (
        (xm_hbm.at[0:W], ua.at[0:W, own]),
        (u_hbm.at[0:2], ua.at[W : W + 2, own]),
        (u_hbm.at[cx - 2 : cx], ua.at[SPAN + W - 1 : SPAN + W + 1, own]),
        (xp_hbm.at[0:W], ua.at[SPAN + W + 1 : 2 * SPAN, own]),
        (xm_hbm.at[W : 2 * W], dd.at[0:W, own]),
        (d_hbm.at[0 : W + 1], dd.at[W:SPAN, own]),
        (d_hbm.at[cx - W - 1 : cx], dd.at[SPAN : SPAN + W + 1, own]),
        (xp_hbm.at[W : 2 * W], dd.at[SPAN + W + 1 : 2 * SPAN, own]),
        (xm_hbm.at[2 * W : 3 * W - 1], rr.at[1:W, own]),
        (r_hbm.at[0 : W + 1], rr.at[W:SPAN, own]),
        (r_hbm.at[cx - W - 1 : cx], rr.at[SPAN : SPAN + W + 1, own]),
        (xp_hbm.at[2 * W : 3 * W - 1], rr.at[SPAN + W + 1 : 2 * SPAN - 1, own]),
        (field_hbm.at[W:8], fin.at[W:8]),
        (field_hbm.at[cx - 8 : cx - W], fin.at[8 : 16 - W]),
    ):
        copies.append(pltpu.make_async_copy(src, dst, sems.at[len(copies)]))
    for copy in copies:
        copy.start()

    rr[0] = jnp.zeros((cy + 8, nz), F32)
    rr[2 * SPAN - 1] = jnp.zeros((cy + 8, nz), F32)

    def rows(dst, plane, after, before):
        dst[plane, cy : cy + W, :] = after
        dst[plane, cy + W : cy + 2 * W, :] = before

    for i in range(W + 1):
        for base, x in ((W + i, i), (SPAN + i, cx - W - 1 + i)):
            for which, dst in enumerate((ua, dd, rr)):
                rows(dst, base, yn[which, x], yp[which, x])
    for side, base in ((0, 0), (1, SPAN + W + 1)):
        at = side * (3 * W - 1)
        for i in range(W):
            rows(ua, base + i, cn[at + i], cp[at + i])
            rows(dd, base + i, cn[at + W + i], cp[at + W + i])
        for i in range(W - 1):
            rows(rr, base + i + 1 - side, cn[at + 2 * W + i], cp[at + 2 * W + i])
    work = Plane(dd, dn, rr, kk, fbuf, place)
    first = (place[0] > 0).astype(F32)
    final = (place[0] < place[2] - 1).astype(F32)
    for copy in copies:
        copy.wait()
    lax.fori_loop(0, dd.shape[0], lambda i, c: (work.prepare(i), c)[1], 0, unroll=2)

    src, dst = ua, ub
    for step in range(STEPS):
        last = step == STEPS - 1

        def end(side, carry, src=src, dst=dst, step=step, last=last):
            base = jnp.where(side == 0, step, SPAN + W - 1 - step)
            for i in range(3):
                work.local(src, dst, base + i)
            work.face(src, base + 1)
            for j in range(W):
                keep = None
                if not last:
                    keep = jnp.where(
                        side == 0, first if j < W - 1 - step else 1.0, final if j > step else 1.0
                    )
                target = side * (16 - W) + j if last else base + 1 + j
                work.across(src, dst, fin if last else dst, base + 1 + j, target, keep)
                if j < W - 1:
                    work.local(src, dst, base + 3 + j)
            return carry

        lax.fori_loop(0, 2, end, 0)
        if not last:
            for i in range(2):
                dst[step + W + 1 + i] = rim[4 * step + i]
                dst[SPAN + W - 2 - step + i] = rim[4 * step + 2 + i]
            src, dst = dst, src
    done = [
        pltpu.make_async_copy(fin.at[0:W], out_hbm.at[0:W], osem.at[0]),
        pltpu.make_async_copy(fin.at[16 - W : 16], out_hbm.at[cx - W : cx], osem.at[1]),
    ]
    for copy in done:
        copy.start()
    turn_over(fin, turned)
    done.append(pltpu.make_async_copy(turned, ft_hbm, osem.at[2]))
    done[2].start()
    for copy in done:
        copy.wait()


def outer(place, u, d, r, yn, yp, xm, xp, cn, cp, rim, field):
    cx, cy, nz = u.shape
    wide = pltpu.VMEM((2 * SPAN, cy + 8, nz), F32)
    return pl.pallas_call(
        outer_kernel,
        out_shape=(
            jax.ShapeDtypeStruct((cx, cy, nz), F32),
            jax.ShapeDtypeStruct((cy, 16, nz), F32),
        ),
        in_specs=[SCALARS] + [ANYWHERE] * 3 + [LOCAL] * 2 + [ANYWHERE] * 2 + [LOCAL] * 3 + [ANYWHERE],
        out_specs=(ANYWHERE, ANYWHERE),
        scratch_shapes=[wide] * 6
        + [
            pltpu.VMEM((cy + 8, nz), F32),
            pltpu.VMEM((16, cy, nz), F32),
            pltpu.VMEM((cy, 16, nz), F32),
            pltpu.SemaphoreType.DMA((14,)),
            pltpu.SemaphoreType.DMA((3,)),
        ],
        input_output_aliases={11: 0},
        name="outer",
    )(place, u, d, r, yn, yp, xm, xp, cn, cp, rim, field)


def render_kernel(whole, part, cen, lev, mix, ft, sign_ref, *rest):
    out, moved = rest[-2:]
    view = pl.program_id(1)
    depth, rows, nz = ft.shape
    blocks = nz // 128
    zero = jnp.zeros((rows, 128), F32)

    @pl.when(view == 0)
    def _():
        lane = lax.broadcasted_iota(jnp.int32, (rows, 128), 1)
        lane_last = lane == 127

        def shear(y, carry):
            cells = [ft[y, :, 128 * b : 128 * b + 128] for b in range(blocks)]
            back = [pltpu.roll(c, 127, 1) for c in cells] + [zero]
            slope = [jnp.where(lane_last, back[b + 1], back[b]) - cells[b] for b in range(blocks)]
            for v in range(VIEWS):
                n, f = whole[v, y], part[v, y]
                turn = lax.rem(128 - n, 128)
                keep = lane < 128 - n
                back = [pltpu.roll(cells[b] + f * slope[b], turn, 1) for b in range(blocks)] + [zero]
                for b in range(blocks):
                    moved[v, y, :, 128 * b : 128 * b + 128] = jnp.where(keep, back[b], back[b + 1])
            return carry

        lax.fori_loop(0, depth, shear, 0, unroll=8)

    for b in range(blocks):
        at = slice(128 * b, 128 * b + 128)
        sign = jnp.broadcast_to(sign_ref[0, :, at], (rows, 128))
        rising = sign < 0.0
        light = jnp.ones((rows, 128), F32)
        sums = [zero] * BUMPS
        for y in range(depth):
            s = moved[view, y, :, at]
            bumps = []
            for i in range(BUMPS):
                t = s - cen[i]
                bumps.append(jnp.exp2(lev[i] - t * t))
            pairs = [bumps[i] + bumps[i + 1] for i in range(0, BUMPS, 2)]
            total = (pairs[0] + pairs[1]) + (pairs[2] + pairs[3])
            after = light * jnp.exp2(total * sign)
            weight = light - after
            light = after
            sums = [sums[i] + bumps[i] * weight for i in range(BUMPS)]
        inverse = 1.0 / light
        through = jnp.where(rising, light, inverse)
        scale = jnp.where(rising, 1.0, -inverse)
        channels = []
        for c in range(3):
            value = mix[c, 0] * sums[0]
            for i in range(1, BUMPS):
                value = value + mix[c, i] * sums[i]
            channels.append(value * scale)
        channels.append(through)
        for d in range(rows // 2):
            out[d, :, at] = jnp.concatenate([c[2 * d : 2 * d + 2] for c in channels], axis=0)


def render(whole, part, cen, lev, mix, ft, signs, spread, count, parts=None):
    cy, cx, nz = ft.shape
    operands = [whole, part, cen, lev, mix, ft, signs]
    in_specs = [SCALARS] * 5 + [
        pl.BlockSpec((cy, 8, nz), lambda i, v: (0, i, 0)),
        pl.BlockSpec((1, 1, nz), lambda i, v: (v, 0, 0)),
    ]
    aliases = {}
    if parts is not None:
        operands.append(parts)
        in_specs.append(ANYWHERE)
        aliases = {7: 0}
    cells = VIEWS * cx * cy * nz
    return pl.pallas_call(
        render_kernel,
        out_shape=jax.ShapeDtypeStruct((count, 8 * VIEWS, nz), F32),
        grid=(cx // 8, VIEWS),
        in_specs=in_specs,
        out_specs=pl.BlockSpec((4, 8, nz), lambda i, v: (spread(i), v, 0)),
        scratch_shapes=[pltpu.VMEM((VIEWS, cy, 8, nz), F32)],
        input_output_aliases=aliases,
        cost_estimate=pl.CostEstimate(
            flops=60 * cells, bytes_accessed=4 * (cx * cy + count * 8 * VIEWS) * nz, transcendentals=9 * cells
        ),
        name="render",
    )(*operands)


def combine_kernel(parts, sign_ref, image, trans):
    count, _, nz = parts.shape
    sub = lax.broadcasted_iota(jnp.int32, (8, nz), 0)
    for view in range(VIEWS):
        rising = jnp.broadcast_to(sign_ref[view], (8, nz)) < 0.0
        total = jnp.zeros((8, nz), F32)
        ahead = jnp.ones((8, nz), F32)
        for source in range(count):
            block = parts[source, 8 * view : 8 * view + 8, :]
            tail = jnp.where(sub >= 6, block, 0.0)
            pair = tail + pltpu.roll(tail, 4, 0)
            light = pair + pltpu.roll(pair, 2, 0)
            total = total * jnp.where(rising, 1.0, light) + block * jnp.where(rising, ahead, 1.0)
            ahead = ahead * light
        for c in range(3):
            image[view, c] = total[2 * c : 2 * c + 2]
        trans[view] = ahead[6:8]


def combine(parts, signs):
    nz = parts.shape[2]
    return pl.pallas_call(
        combine_kernel,
        out_shape=(
            jax.ShapeDtypeStruct((VIEWS, 3, 2, nz), F32),
            jax.ShapeDtypeStruct((VIEWS, 2, nz), F32),
        ),
        name="combine",
    )(parts, signs)


def scene_of(u, d, r, offsets, depth_order, centres, colour, opacity):
    cx, cy, _ = u.shape
    place = jnp.stack(
        [
            lax.axis_index("sx"),
            lax.axis_index("sy"),
            jnp.int32(lax.axis_size("sx")),
            jnp.int32(lax.axis_size("sy")),
        ]
    ).astype(jnp.int32)
    up_x = jnp.concatenate([u[cx - W :], d[cx - W :], r[cx - W + 1 :]])
    down_x = jnp.concatenate([u[:W], d[:W], r[: W - 1]])
    xm = shift(up_x, "sx", True)
    xp = shift(down_x, "sx", False)
    up_y = jnp.stack([a[:, cy - W :] for a in (u, d, r)])
    down_y = jnp.stack([a[:, :W] for a in (u, d, r)])
    yp = shift(up_y, "sy", True)
    yn = shift(down_y, "sy", False)
    cp = shift(jnp.concatenate([xm[:, cy - W :], xp[:, cy - W :]]), "sy", True)
    cn = shift(jnp.concatenate([xm[:, :W], xp[:, :W]]), "sy", False)
    offs = lax.dynamic_slice_in_dim(offsets, lax.axis_index("sy") * cy, cy, 1)
    signs = jnp.where(depth_order == 0, -1.0, 1.0).astype(F32)[:, None, :]
    level = opacity * LOG2E
    scene = (offs // 4, (offs % 4).astype(F32) * 0.25, centres * GAIN, jnp.log2(level), colour / level)

    field, turned, rim = inner(place, u, d, r, yn, yp)
    parts = render(*scene, turned, signs, lambda i: i + 1, cx // 2)
    field, turned = outer(place, u, d, r, yn, yp, xm, xp, cn, cp, rim, field)
    parts = render(*scene, turned, signs, lambda i: 3 * i, cx // 2, parts)
    parts = lax.all_to_all(parts, "sy", split_axis=0, concat_axis=0, tiled=True)
    image, trans = combine(parts, signs)
    return field, image, trans


def solution(mesh):
    grid = P("sx", "sy", None)
    return jax.shard_map(
        scene_of,
        mesh=mesh,
        in_specs=(grid, grid, grid, P(), P(), P(), P(), P()),
        out_specs=(
            grid,
            P(None, None, ("sx", "sy"), None),
            P(None, ("sx", "sy"), None),
        ),
        check_vma=False,
    )
```

```python
import jax
import jax.numpy as jnp
from jax import lax
from jax.experimental import pallas as pl
from jax.experimental.pallas import tpu as pltpu
from jax.sharding import PartitionSpec as P


STEPS = 4
VIEWS = 4
BUMPS = 8
W = STEPS
LOG2E = 1.4426950408889634
GAIN = 2.0 * LOG2E**0.5

F32 = jnp.float32


def shift(value, axis, up):
    size = lax.axis_size(axis)
    pairs = [(i, i + 1) for i in range(size - 1)]
    if not up:
        pairs = [(j, i) for i, j in pairs]
    return lax.ppermute(value, axis, pairs)


ANYWHERE = pl.BlockSpec(memory_space=pl.ANY)
LOCAL = pl.BlockSpec(memory_space=pltpu.VMEM)
SCALARS = pl.BlockSpec(memory_space=pltpu.SMEM)


def rows_kernel(u_hbm, d_hbm, r_hbm, up, down, low, high, sems):
    cx, cy = u_hbm.shape[0], u_hbm.shape[1]
    copies = []
    for which, src in enumerate((u_hbm, d_hbm, r_hbm)):
        for dst, first in ((low, 0), (high, cy - 8)):
            copies.append(
                pltpu.make_async_copy(
                    src.at[:, first : first + 8], dst.at[which], sems.at[len(copies)]
                )
            )
    for copy in copies:
        copy.start()
    for which in range(3):
        copies[2 * which].wait()
        copies[2 * which + 1].wait()

        def body(x, carry, which=which):
            down[which, x] = low[which, x, 0:W, :]
            up[which, x] = high[which, x, 8 - W : 8, :]
            return carry

        lax.fori_loop(0, cx, body, 0, unroll=4)


def rows_of(u, d, r):
    cx, _, nz = u.shape
    message = jax.ShapeDtypeStruct((3, cx, W, nz), F32)
    return pl.pallas_call(
        rows_kernel,
        out_shape=(message, message),
        in_specs=[ANYWHERE] * 3,
        out_specs=(LOCAL, LOCAL),
        scratch_shapes=[
            pltpu.VMEM((3, cx, 8, nz), F32),
            pltpu.VMEM((3, cx, 8, nz), F32),
            pltpu.SemaphoreType.DMA((6,)),
        ],
        name="rows",
    )(u, d, r)


def planes_kernel(u_hbm, d_hbm, r_hbm, up, down, sems):
    cx = u_hbm.shape[0]
    copies = []
    for src, first, count in ((u_hbm, 0, W), (d_hbm, W, W), (r_hbm, 2 * W, W - 1)):
        for dst, start in ((up, cx - count), (down, 0)):
            copies.append(
                pltpu.make_async_copy(
                    src.at[start : start + count],
                    dst.at[first : first + count],
                    sems.at[len(copies)],
                )
            )
    for copy in copies:
        copy.start()
    for copy in copies:
        copy.wait()


def planes_of(u, d, r):
    _, cy, nz = u.shape
    message = jax.ShapeDtypeStruct((3 * W - 1, cy, nz), F32)
    return pl.pallas_call(
        planes_kernel,
        out_shape=(message, message),
        in_specs=[ANYWHERE] * 3,
        out_specs=(LOCAL, LOCAL),
        scratch_shapes=[pltpu.SemaphoreType.DMA((6,))],
        name="planes",
    )(u, d, r)


def cut(tile, block):
    return (slice(8 * tile, 8 * tile + 8), slice(128 * block, 128 * block + 128))


class Plane:
    def __init__(self, dd, dn, rr, kk, fbuf):
        self.dd, self.dn, self.rr, self.kk, self.fbuf = dd, dn, rr, kk, fbuf
        self.tiles, self.blocks = dd.shape[1] // 8, dd.shape[2] // 128
        sub = lax.broadcasted_iota(jnp.int32, (8, 128), 0)
        lane = lax.broadcasted_iota(jnp.int32, (8, 128), 1)
        self.sub_last, self.sub_first = sub == 7, sub == 0
        self.lane_last, self.lane_first = lane == 127, lane == 0
        self.zero = jnp.zeros((8, 128), F32)
        sy = lax.axis_index("sy")
        self.inside = jnp.where(
            sub < W, (sy < lax.axis_size("sy") - 1).astype(F32), (sy > 0).astype(F32)
        )

    def prepare(self, plane):
        for t in range(self.tiles):
            up = [pltpu.roll(self.dd[(plane,) + cut(t, b)], 127, 1) for b in range(self.blocks)]
            up.append(self.zero)
            for b in range(self.blocks):
                self.dn[(plane,) + cut(t, b)] = jnp.where(self.lane_last, up[b + 1], up[b])

    def local(self, src, dst, plane):
        blocks = self.blocks
        for t in range(self.tiles):
            u = [src[(plane,) + cut(t, b)] for b in range(blocks)]
            warm = [jnp.tanh(v) for v in u]
            k = [self.dd[(plane,) + cut(t, b)] * (0.5 + 0.2 * warm[b]) for b in range(blocks)]
            u_up = [pltpu.roll(v, 127, 1) for v in u] + [self.zero]
            flux = []
            for b in range(blocks):
                un = jnp.where(self.lane_last, u_up[b + 1], u_up[b])
                kn = self.dn[(plane,) + cut(t, b)] * (0.5 + 0.2 * jnp.tanh(un))
                flux.append((k[b] + kn) * (un - u[b]))
            down = [pltpu.roll(v, 1, 1) for v in flux]
            for b in range(blocks):
                at = (plane,) + cut(t, b)
                low = jnp.where(self.lane_first, k[b] * u[b] if b == 0 else down[b - 1], down[b])
                self.kk[at] = k[b]
                dst[at] = u[b] + ((flux[b] - low) + self.rr[at] * warm[b])

    def face(self, src, plane):
        for t in range(self.tiles):
            for b in range(self.blocks):
                at = cut(t, b)
                self.fbuf[at] = (self.kk[(plane - 1,) + at] + self.kk[(plane,) + at]) * (
                    src[(plane,) + at] - src[(plane - 1,) + at]
                )

    def across(self, src, base, dst, plane, target, keep=None):
        tiles, kk = self.tiles, self.kk
        for b in range(self.blocks):
            u = [src[(plane,) + cut(t, b)] for t in range(tiles)]
            k = [kk[(plane,) + cut(t, b)] for t in range(tiles)]
            u_up = [pltpu.roll(v, 7, 0) for v in u]
            k_up = [pltpu.roll(v, 7, 0) for v in k]
            flux = []
            for t in range(tiles):
                n = (t + 1) % tiles
                un = jnp.where(self.sub_last, u_up[n], u_up[t])
                kn = jnp.where(self.sub_last, k_up[n], k_up[t])
                flux.append((k[t] + kn) * (un - u[t]))
            down = [pltpu.roll(v, 1, 0) for v in flux]
            for t in range(min(tiles, dst.shape[1] // 8)):
                at = cut(t, b)
                change = flux[t] - jnp.where(self.sub_first, down[t - 1], down[t])
                fx = (k[t] + kk[(plane + 1,) + at]) * (src[(plane + 1,) + at] - u[t])
                new = base[(plane,) + at] + (change + (fx - self.fbuf[at]))
                self.fbuf[at] = fx
                if t == tiles - 1:
                    new = new * self.inside
                if keep is not None:
                    new = new * keep
                dst[(target,) + at] = new


def turn_over(field, turned):
    cx, cy, nz = field.shape[0], field.shape[1], field.shape[2]

    def group(xg, carry):
        rows = pl.ds(pl.multiple_of(8 * xg, 8), 8)
        for yg in range(cy // 8):
            for b in range(nz // 128):
                columns = slice(128 * b, 128 * b + 128)
                piece = field[rows, 8 * yg : 8 * yg + 8, columns]
                turned[8 * yg : 8 * yg + 8, rows, columns] = jnp.transpose(piece, (1, 0, 2)) * GAIN
        return carry

    lax.fori_loop(0, cx // 8, group, 0)


def inner_kernel(
    u_hbm, d_hbm, r_hbm, yn, yp,
    out_hbm, ft_hbm, rim,
    ua, ub, dd, dn, rr, kk, fbuf, fin, turned, sems, osem,
):
    cx, cy, _ = u_hbm.shape
    copies = [
        pltpu.make_async_copy(src, dst.at[:, 0:cy], sems.at[i])
        for i, (src, dst) in enumerate(((u_hbm, ua), (d_hbm, dd), (r_hbm, rr)))
    ]
    for copy in copies:
        copy.start()

    def edge_rows(x, carry):
        for which, dst in enumerate((ua, dd, rr)):
            dst[x, cy : cy + W, :] = yn[which, x]
            dst[x, cy + W : cy + 2 * W, :] = yp[which, x]
        return carry

    lax.fori_loop(0, cx, edge_rows, 0)
    work = Plane(dd, dn, rr, kk, fbuf)
    for copy in copies:
        copy.wait()
    lax.fori_loop(0, dd.shape[0], lambda i, c: (work.prepare(i), c)[1], 0, unroll=2)

    src, dst = ua, ub
    for step in range(STEPS):
        last = step == STEPS - 1
        low, high = step + 1, cx - 1 - step
        for plane in range(3):
            work.local(src, dst, low - 1 + plane)
        work.face(src, low)

        def body(plane, carry, src=src, dst=dst, last=last, high=high):
            work.across(
                src, dst, fin if last else dst, plane, plane - W if last else plane
            )
            work.local(src, dst, jnp.minimum(plane + 2, high))
            return carry

        lax.fori_loop(low, high, body, 0)
        if not last:
            for i, plane in enumerate((low, low + 1, high - 2, high - 1)):
                rim[4 * step + i] = dst[plane]
            src, dst = dst, src
    done = pltpu.make_async_copy(fin, out_hbm.at[W : cx - W], osem.at[0])
    done.start()
    turn_over(fin.at[8 - W : cx - 8 - W], turned)
    move = pltpu.make_async_copy(turned, ft_hbm, osem.at[1])
    move.start()
    done.wait()
    move.wait()


def inner(u, d, r, yn, yp):
    cx, cy, nz = u.shape
    wide = pltpu.VMEM((cx, cy + 8, nz), F32)
    return pl.pallas_call(
        inner_kernel,
        out_shape=(
            jax.ShapeDtypeStruct((cx, cy, nz), F32),
            jax.ShapeDtypeStruct((cy, cx - 16, nz), F32),
            jax.ShapeDtypeStruct((4 * (STEPS - 1), cy + 8, nz), F32),
        ),
        in_specs=[ANYWHERE] * 3 + [LOCAL] * 2,
        out_specs=(ANYWHERE, ANYWHERE, LOCAL),
        scratch_shapes=[wide] * 6
        + [
            pltpu.VMEM((cy + 8, nz), F32),
            pltpu.VMEM((cx - 2 * W, cy, nz), F32),
            pltpu.VMEM((cy, cx - 16, nz), F32),
            pltpu.SemaphoreType.DMA((3,)),
            pltpu.SemaphoreType.DMA((2,)),
        ],
        cost_estimate=pl.CostEstimate(
            flops=40 * STEPS * cx * cy * nz, bytes_accessed=24 * cx * cy * nz, transcendentals=0
        ),
        name="inner",
    )(u, d, r, yn, yp)


SPAN = 2 * W + 1


def outer_kernel(
    u_hbm, d_hbm, r_hbm, yn, yp, xm_hbm, xp_hbm, cn, cp, rim, field_hbm,
    out_hbm, ft_hbm,
    ua, ub, dd, dn, rr, kk, fbuf, fin, turned, sems, osem,
):
    cx, cy, nz = u_hbm.shape
    own = slice(0, cy)
    copies = []
    for src, dst in (
        (xm_hbm.at[0:W], ua.at[0:W, own]),
        (u_hbm.at[0:2], ua.at[W : W + 2, own]),
        (u_hbm.at[cx - 2 : cx], ua.at[SPAN + W - 1 : SPAN + W + 1, own]),
        (xp_hbm.at[0:W], ua.at[SPAN + W + 1 : 2 * SPAN, own]),
        (xm_hbm.at[W : 2 * W], dd.at[0:W, own]),
        (d_hbm.at[0 : W + 1], dd.at[W:SPAN, own]),
        (d_hbm.at[cx - W - 1 : cx], dd.at[SPAN : SPAN + W + 1, own]),
        (xp_hbm.at[W : 2 * W], dd.at[SPAN + W + 1 : 2 * SPAN, own]),
        (xm_hbm.at[2 * W : 3 * W - 1], rr.at[1:W, own]),
        (r_hbm.at[0 : W + 1], rr.at[W:SPAN, own]),
        (r_hbm.at[cx - W - 1 : cx], rr.at[SPAN : SPAN + W + 1, own]),
        (xp_hbm.at[2 * W : 3 * W - 1], rr.at[SPAN + W + 1 : 2 * SPAN - 1, own]),
        (field_hbm.at[W:8], fin.at[W:8]),
        (field_hbm.at[cx - 8 : cx - W], fin.at[8 : 16 - W]),
    ):
        copies.append(pltpu.make_async_copy(src, dst, sems.at[len(copies)]))
    for copy in copies:
        copy.start()

    rr[0] = jnp.zeros((cy + 8, nz), F32)
    rr[2 * SPAN - 1] = jnp.zeros((cy + 8, nz), F32)

    def rows(dst, plane, after, before):
        dst[plane, cy : cy + W, :] = after
        dst[plane, cy + W : cy + 2 * W, :] = before

    for i in range(W + 1):
        for base, x in ((W + i, i), (SPAN + i, cx - W - 1 + i)):
            for which, dst in enumerate((ua, dd, rr)):
                rows(dst, base, yn[which, x], yp[which, x])
    for side, base in ((0, 0), (1, SPAN + W + 1)):
        at = side * (3 * W - 1)
        for i in range(W):
            rows(ua, base + i, cn[at + i], cp[at + i])
            rows(dd, base + i, cn[at + W + i], cp[at + W + i])
        for i in range(W - 1):
            rows(rr, base + i + 1 - side, cn[at + 2 * W + i], cp[at + 2 * W + i])
    work = Plane(dd, dn, rr, kk, fbuf)
    sx = lax.axis_index("sx")
    first = (sx > 0).astype(F32)
    final = (sx < lax.axis_size("sx") - 1).astype(F32)
    for copy in copies:
        copy.wait()
    lax.fori_loop(0, dd.shape[0], lambda i, c: (work.prepare(i), c)[1], 0, unroll=2)

    src, dst = ua, ub
    for step in range(STEPS):
        last = step == STEPS - 1

        def end(side, carry, src=src, dst=dst, step=step, last=last):
            base = jnp.where(side == 0, step, SPAN + W - 1 - step)
            for i in range(3):
                work.local(src, dst, base + i)
            work.face(src, base + 1)
            for j in range(W):
                keep = None
                if not last:
                    keep = jnp.where(
                        side == 0, first if j < W - 1 - step else 1.0, final if j > step else 1.0
                    )
                target = side * (16 - W) + j if last else base + 1 + j
                work.across(src, dst, fin if last else dst, base + 1 + j, target, keep)
                if j < W - 1:
                    work.local(src, dst, base + 3 + j)
            return carry

        lax.fori_loop(0, 2, end, 0)
        if not last:
            for i in range(2):
                dst[step + W + 1 + i] = rim[4 * step + i]
                dst[SPAN + W - 2 - step + i] = rim[4 * step + 2 + i]
            src, dst = dst, src
    done = [
        pltpu.make_async_copy(fin.at[0:W], out_hbm.at[0:W], osem.at[0]),
        pltpu.make_async_copy(fin.at[16 - W : 16], out_hbm.at[cx - W : cx], osem.at[1]),
    ]
    for copy in done:
        copy.start()
    turn_over(fin, turned)
    done.append(pltpu.make_async_copy(turned, ft_hbm, osem.at[2]))
    done[2].start()
    for copy in done:
        copy.wait()


def outer(u, d, r, yn, yp, xm, xp, cn, cp, rim, field):
    cx, cy, nz = u.shape
    wide = pltpu.VMEM((2 * SPAN, cy + 8, nz), F32)
    return pl.pallas_call(
        outer_kernel,
        out_shape=(
            jax.ShapeDtypeStruct((cx, cy, nz), F32),
            jax.ShapeDtypeStruct((cy, 16, nz), F32),
        ),
        in_specs=[ANYWHERE] * 3 + [LOCAL] * 2 + [ANYWHERE] * 2 + [LOCAL] * 3 + [ANYWHERE],
        out_specs=(ANYWHERE, ANYWHERE),
        scratch_shapes=[wide] * 6
        + [
            pltpu.VMEM((cy + 8, nz), F32),
            pltpu.VMEM((16, cy, nz), F32),
            pltpu.VMEM((cy, 16, nz), F32),
            pltpu.SemaphoreType.DMA((14,)),
            pltpu.SemaphoreType.DMA((3,)),
        ],
        input_output_aliases={10: 0},
        name="outer",
    )(u, d, r, yn, yp, xm, xp, cn, cp, rim, field)


def render_kernel(offs, scene, order, ft, *rest):
    out, moved = rest[-2:]
    view = pl.program_id(1)
    depth, rows, nz = ft.shape
    blocks = nz // 128
    zero = jnp.zeros((rows, 128), F32)

    @pl.when(view == 0)
    def _():
        lane = lax.broadcasted_iota(jnp.int32, (rows, 128), 1)
        lane_last = lane == 127

        def shear(y, carry):
            cells = [ft[y, :, 128 * b : 128 * b + 128] for b in range(blocks)]
            back = [pltpu.roll(c, 127, 1) for c in cells] + [zero]
            slope = [jnp.where(lane_last, back[b + 1], back[b]) - cells[b] for b in range(blocks)]
            for v in range(VIEWS):
                q = offs[v, lax.axis_index("sy") * depth + y]
                n = lax.div(q, 4)
                f = (q - 4 * n).astype(F32) * 0.25
                turn = lax.rem(128 - n, 128)
                keep = lane < 128 - n
                back = [pltpu.roll(cells[b] + f * slope[b], turn, 1) for b in range(blocks)] + [zero]
                for b in range(blocks):
                    moved[v, y, :, 128 * b : 128 * b + 128] = jnp.where(keep, back[b], back[b + 1])
            return carry

        lax.fori_loop(0, depth, shear, 0, unroll=8)

    for b in range(blocks):
        at = slice(128 * b, 128 * b + 128)
        side = jnp.broadcast_to(order[0:1, at], (rows, 128))
        for v in range(1, VIEWS):
            side = jnp.where(view == v, jnp.broadcast_to(order[v : v + 1, at], (rows, 128)), side)
        sign = jnp.where(side == 0, -1.0, 1.0)
        rising = sign < 0.0
        light = jnp.ones((rows, 128), F32)
        sums = [zero] * BUMPS
        for y in range(depth):
            s = moved[view, y, :, at]
            bumps = []
            for i in range(BUMPS):
                t = s - scene[0, i]
                bumps.append(jnp.exp2(scene[1, i] - t * t))
            pairs = [bumps[i] + bumps[i + 1] for i in range(0, BUMPS, 2)]
            total = (pairs[0] + pairs[1]) + (pairs[2] + pairs[3])
            after = light * jnp.exp2(total * sign)
            weight = light - after
            light = after
            sums = [sums[i] + bumps[i] * weight for i in range(BUMPS)]
        inverse = 1.0 / light
        through = jnp.where(rising, light, inverse)
        scale = jnp.where(rising, 1.0, -inverse)
        channels = []
        for c in range(3):
            value = scene[2 + c, 0] * sums[0]
            for i in range(1, BUMPS):
                value = value + scene[2 + c, i] * sums[i]
            channels.append(value * scale)
        channels.append(through)
        for d in range(rows // 2):
            out[d, :, at] = jnp.concatenate([c[2 * d : 2 * d + 2] for c in channels], axis=0)


def render(offs, scene, order, ft, spread, count, parts=None):
    cy, cx, nz = ft.shape
    operands = [offs, scene, order, ft]
    in_specs = [SCALARS] * 2 + [
        pl.BlockSpec((VIEWS, nz), lambda i, v: (0, 0)),
        pl.BlockSpec((cy, 8, nz), lambda i, v: (0, i, 0)),
    ]
    aliases = {}
    if parts is not None:
        operands.append(parts)
        in_specs.append(ANYWHERE)
        aliases = {4: 0}
    cells = VIEWS * cx * cy * nz
    return pl.pallas_call(
        render_kernel,
        out_shape=jax.ShapeDtypeStruct((count, 8 * VIEWS, nz), F32),
        grid=(cx // 8, VIEWS),
        in_specs=in_specs,
        out_specs=pl.BlockSpec((4, 8, nz), lambda i, v: (spread(i), v, 0)),
        scratch_shapes=[pltpu.VMEM((VIEWS, cy, 8, nz), F32)],
        input_output_aliases=aliases,
        cost_estimate=pl.CostEstimate(
            flops=60 * cells, bytes_accessed=4 * (cx * cy + count * 8 * VIEWS) * nz, transcendentals=9 * cells
        ),
        name="render",
    )(*operands)


def combine_kernel(parts, order, image, trans):
    count, _, nz = parts.shape
    sub = lax.broadcasted_iota(jnp.int32, (8, nz), 0)
    for view in range(VIEWS):
        rising = jnp.broadcast_to(order[view : view + 1, :], (8, nz)) == 0
        total = jnp.zeros((8, nz), F32)
        ahead = jnp.ones((8, nz), F32)
        for source in range(count):
            block = parts[source, 8 * view : 8 * view + 8, :]
            tail = jnp.where(sub >= 6, block, 0.0)
            pair = tail + pltpu.roll(tail, 4, 0)
            light = pair + pltpu.roll(pair, 2, 0)
            total = total * jnp.where(rising, 1.0, light) + block * jnp.where(rising, ahead, 1.0)
            ahead = ahead * light
        for c in range(3):
            image[view, c] = total[2 * c : 2 * c + 2]
        trans[view] = ahead[6:8]


def combine(parts, order):
    nz = parts.shape[2]
    return pl.pallas_call(
        combine_kernel,
        out_shape=(
            jax.ShapeDtypeStruct((VIEWS, 3, 2, nz), F32),
            jax.ShapeDtypeStruct((VIEWS, 2, nz), F32),
        ),
        name="combine",
    )(parts, order)


def scene_of(u, d, r, offsets, depth_order, centres, colour, opacity):
    cx, cy, _ = u.shape
    up_y, down_y = rows_of(u, d, r)
    yp = shift(up_y, "sy", True)
    yn = shift(down_y, "sy", False)
    up_x, down_x = planes_of(u, d, r)
    xm = shift(up_x, "sx", True)
    xp = shift(down_x, "sx", False)
    cp = shift(jnp.concatenate([xm[:, cy - W :], xp[:, cy - W :]]), "sy", True)
    cn = shift(jnp.concatenate([xm[:, :W], xp[:, :W]]), "sy", False)
    level = opacity * LOG2E
    scene = jnp.concatenate([(centres * GAIN)[None], jnp.log2(level)[None], colour / level])

    field, turned, rim = inner(u, d, r, yn, yp)
    parts = render(offsets, scene, depth_order, turned, lambda i: i + 1, cx // 2)
    field, turned = outer(u, d, r, yn, yp, xm, xp, cn, cp, rim, field)
    parts = render(offsets, scene, depth_order, turned, lambda i: 3 * i, cx // 2, parts)
    parts = lax.all_to_all(parts, "sy", split_axis=0, concat_axis=0, tiled=True)
    image, trans = combine(parts, depth_order)
    return field, image, trans


def solution(mesh):
    grid = P("sx", "sy", None)
    return jax.shard_map(
        scene_of,
        mesh=mesh,
        in_specs=(grid, grid, grid, P(), P(), P(), P(), P()),
        out_specs=(
            grid,
            P(None, None, ("sx", "sy"), None),
            P(None, ("sx", "sy"), None),
        ),
        check_vma=False,
    )
```

```python
import jax
import jax.numpy as jnp
from jax import lax
from jax.experimental import pallas as pl
from jax.experimental.pallas import tpu as pltpu
from jax.sharding import PartitionSpec as P


STEPS = 4
VIEWS = 4
BUMPS = 8
W = STEPS
LOG2E = 1.4426950408889634
GAIN = 2.0 * LOG2E**0.5

F32 = jnp.float32


def shift(value, axis, up):
    size = lax.axis_size(axis)
    pairs = [(i, i + 1) for i in range(size - 1)]
    if not up:
        pairs = [(j, i) for i, j in pairs]
    return lax.ppermute(value, axis, pairs)


ANYWHERE = pl.BlockSpec(memory_space=pl.ANY)
LOCAL = pl.BlockSpec(memory_space=pltpu.VMEM)
SCALARS = pl.BlockSpec(memory_space=pltpu.SMEM)


def rows_kernel(u_hbm, d_hbm, r_hbm, up, down, low, high, sems):
    cx, cy = u_hbm.shape[0], u_hbm.shape[1]
    copies = []
    for which, src in enumerate((u_hbm, d_hbm, r_hbm)):
        for dst, first in ((low, 0), (high, cy - 8)):
            copies.append(
                pltpu.make_async_copy(
                    src.at[:, first : first + 8], dst.at[which], sems.at[len(copies)]
                )
            )
    for copy in copies:
        copy.start()
    for which in range(3):
        copies[2 * which].wait()
        copies[2 * which + 1].wait()

        def body(x, carry, which=which):
            down[which, x] = low[which, x, 0:W, :]
            up[which, x] = high[which, x, 8 - W : 8, :]
            return carry

        lax.fori_loop(0, cx, body, 0, unroll=4)


def rows_of(u, d, r):
    cx, _, nz = u.shape
    message = jax.ShapeDtypeStruct((3, cx, W, nz), F32)
    return pl.pallas_call(
        rows_kernel,
        out_shape=(message, message),
        in_specs=[ANYWHERE] * 3,
        out_specs=(LOCAL, LOCAL),
        scratch_shapes=[
            pltpu.VMEM((3, cx, 8, nz), F32),
            pltpu.VMEM((3, cx, 8, nz), F32),
            pltpu.SemaphoreType.DMA((6,)),
        ],
        name="rows",
    )(u, d, r)


def planes_kernel(u_hbm, d_hbm, r_hbm, up, down, sems):
    cx = u_hbm.shape[0]
    copies = []
    for src, first, count in ((u_hbm, 0, W), (d_hbm, W, W), (r_hbm, 2 * W, W - 1)):
        for dst, start in ((up, cx - count), (down, 0)):
            copies.append(
                pltpu.make_async_copy(
                    src.at[start : start + count],
                    dst.at[first : first + count],
                    sems.at[len(copies)],
                )
            )
    for copy in copies:
        copy.start()
    for copy in copies:
        copy.wait()


def planes_of(u, d, r):
    _, cy, nz = u.shape
    message = jax.ShapeDtypeStruct((3 * W - 1, cy, nz), F32)
    return pl.pallas_call(
        planes_kernel,
        out_shape=(message, message),
        in_specs=[ANYWHERE] * 3,
        out_specs=(LOCAL, LOCAL),
        scratch_shapes=[pltpu.SemaphoreType.DMA((6,))],
        name="planes",
    )(u, d, r)


def cut(tile, block):
    return (slice(8 * tile, 8 * tile + 8), slice(128 * block, 128 * block + 128))


class Plane:
    def __init__(self, dd, dn, rr, kk, fbuf):
        self.dd, self.dn, self.rr, self.kk, self.fbuf = dd, dn, rr, kk, fbuf
        self.tiles, self.blocks = dd.shape[1] // 8, dd.shape[2] // 128
        sub = lax.broadcasted_iota(jnp.int32, (8, 128), 0)
        lane = lax.broadcasted_iota(jnp.int32, (8, 128), 1)
        self.sub_last, self.sub_first = sub == 7, sub == 0
        self.lane_last, self.lane_first = lane == 127, lane == 0
        self.zero = jnp.zeros((8, 128), F32)
        sy = lax.axis_index("sy")
        self.inside = jnp.where(
            sub < W, (sy < lax.axis_size("sy") - 1).astype(F32), (sy > 0).astype(F32)
        )

    def prepare(self, plane):
        for t in range(self.tiles):
            up = [pltpu.roll(self.dd[(plane,) + cut(t, b)], 127, 1) for b in range(self.blocks)]
            up.append(self.zero)
            for b in range(self.blocks):
                self.dn[(plane,) + cut(t, b)] = jnp.where(self.lane_last, up[b + 1], up[b])

    def local(self, src, dst, plane):
        blocks = self.blocks
        for t in range(self.tiles):
            u = [src[(plane,) + cut(t, b)] for b in range(blocks)]
            warm = [jnp.tanh(v) for v in u]
            k = [self.dd[(plane,) + cut(t, b)] * (0.5 + 0.2 * warm[b]) for b in range(blocks)]
            u_up = [pltpu.roll(v, 127, 1) for v in u] + [self.zero]
            flux = []
            for b in range(blocks):
                un = jnp.where(self.lane_last, u_up[b + 1], u_up[b])
                kn = self.dn[(plane,) + cut(t, b)] * (0.5 + 0.2 * jnp.tanh(un))
                flux.append((k[b] + kn) * (un - u[b]))
            down = [pltpu.roll(v, 1, 1) for v in flux]
            for b in range(blocks):
                at = (plane,) + cut(t, b)
                low = jnp.where(self.lane_first, k[b] * u[b] if b == 0 else down[b - 1], down[b])
                self.kk[at] = k[b]
                dst[at] = u[b] + ((flux[b] - low) + self.rr[at] * warm[b])

    def face(self, src, plane):
        for t in range(self.tiles):
            for b in range(self.blocks):
                at = cut(t, b)
                self.fbuf[at] = (self.kk[(plane - 1,) + at] + self.kk[(plane,) + at]) * (
                    src[(plane,) + at] - src[(plane - 1,) + at]
                )

    def across(self, src, base, dst, plane, target, keep=None):
        tiles, kk = self.tiles, self.kk
        for b in range(self.blocks):
            u = [src[(plane,) + cut(t, b)] for t in range(tiles)]
            k = [kk[(plane,) + cut(t, b)] for t in range(tiles)]
            u_up = [pltpu.roll(v, 7, 0) for v in u]
            k_up = [pltpu.roll(v, 7, 0) for v in k]
            flux = []
            for t in range(tiles):
                n = (t + 1) % tiles
                un = jnp.where(self.sub_last, u_up[n], u_up[t])
                kn = jnp.where(self.sub_last, k_up[n], k_up[t])
                flux.append((k[t] + kn) * (un - u[t]))
            down = [pltpu.roll(v, 1, 0) for v in flux]
            for t in range(min(tiles, dst.shape[1] // 8)):
                at = cut(t, b)
                change = flux[t] - jnp.where(self.sub_first, down[t - 1], down[t])
                fx = (k[t] + kk[(plane + 1,) + at]) * (src[(plane + 1,) + at] - u[t])
                new = base[(plane,) + at] + (change + (fx - self.fbuf[at]))
                self.fbuf[at] = fx
                if t == tiles - 1:
                    new = new * self.inside
                if keep is not None:
                    new = new * keep
                dst[(target,) + at] = new


def turn_over(field, turned):
    cx, cy, nz = field.shape[0], field.shape[1], field.shape[2]

    def group(xg, carry):
        rows = pl.ds(pl.multiple_of(8 * xg, 8), 8)
        for yg in range(cy // 8):
            for b in range(nz // 128):
                columns = slice(128 * b, 128 * b + 128)
                piece = field[rows, 8 * yg : 8 * yg + 8, columns]
                turned[8 * yg : 8 * yg + 8, rows, columns] = jnp.transpose(piece, (1, 0, 2)) * GAIN
        return carry

    lax.fori_loop(0, cx // 8, group, 0)


def inner_kernel(
    u_hbm, d_hbm, r_hbm, yn, yp,
    out_hbm, ft_hbm, rim,
    ua, ub, dd, dn, rr, kk, fbuf, fin, turned, sems, osem,
):
    cx, cy, _ = u_hbm.shape
    copies = [
        pltpu.make_async_copy(src, dst.at[:, 0:cy], sems.at[i])
        for i, (src, dst) in enumerate(((u_hbm, ua), (d_hbm, dd), (r_hbm, rr)))
    ]
    for copy in copies:
        copy.start()

    def edge_rows(x, carry):
        for which, dst in enumerate((ua, dd, rr)):
            dst[x, cy : cy + W, :] = yn[which, x]
            dst[x, cy + W : cy + 2 * W, :] = yp[which, x]
        return carry

    lax.fori_loop(0, cx, edge_rows, 0)
    work = Plane(dd, dn, rr, kk, fbuf)
    for copy in copies:
        copy.wait()
    lax.fori_loop(0, dd.shape[0], lambda i, c: (work.prepare(i), c)[1], 0, unroll=2)

    src, dst = ua, ub
    for step in range(STEPS):
        last = step == STEPS - 1
        low, high = step + 1, cx - 1 - step
        for plane in range(3):
            work.local(src, dst, low - 1 + plane)
        work.face(src, low)

        def body(plane, carry, src=src, dst=dst, last=last, high=high):
            work.across(
                src, dst, fin if last else dst, plane, plane - W if last else plane
            )
            work.local(src, dst, jnp.minimum(plane + 2, high))
            return carry

        lax.fori_loop(low, high, body, 0)
        if not last:
            for i, plane in enumerate((low, low + 1, high - 2, high - 1)):
                rim[4 * step + i] = dst[plane]
            src, dst = dst, src
    done = pltpu.make_async_copy(fin, out_hbm.at[W : cx - W], osem.at[0])
    done.start()
    turn_over(fin.at[8 - W : cx - 8 - W], turned)
    move = pltpu.make_async_copy(turned, ft_hbm, osem.at[1])
    move.start()
    done.wait()
    move.wait()


def inner(u, d, r, yn, yp):
    cx, cy, nz = u.shape
    wide = pltpu.VMEM((cx, cy + 8, nz), F32)
    return pl.pallas_call(
        inner_kernel,
        out_shape=(
            jax.ShapeDtypeStruct((cx, cy, nz), F32),
            jax.ShapeDtypeStruct((cy, cx - 16, nz), F32),
            jax.ShapeDtypeStruct((4 * (STEPS - 1), cy + 8, nz), F32),
        ),
        in_specs=[ANYWHERE] * 3 + [LOCAL] * 2,
        out_specs=(ANYWHERE, ANYWHERE, LOCAL),
        scratch_shapes=[wide] * 6
        + [
            pltpu.VMEM((cy + 8, nz), F32),
            pltpu.VMEM((cx - 2 * W, cy, nz), F32),
            pltpu.VMEM((cy, cx - 16, nz), F32),
            pltpu.SemaphoreType.DMA((3,)),
            pltpu.SemaphoreType.DMA((2,)),
        ],
        cost_estimate=pl.CostEstimate(
            flops=40 * STEPS * cx * cy * nz, bytes_accessed=24 * cx * cy * nz, transcendentals=0
        ),
        name="inner",
    )(u, d, r, yn, yp)


SPAN = 2 * W + 1


def outer_kernel(
    u_hbm, d_hbm, r_hbm, yn, yp, xm_hbm, xp_hbm, cn, cp, rim, offs, scene, order, field_hbm, parts_hbm,
    out_hbm, all_hbm,
    ua, ub, dd, dn, rr, kk, fbuf, fin, turned, moved, parts, sems, osem,
):
    cx, cy, nz = u_hbm.shape
    own = slice(0, cy)
    copies = []
    for src, dst in (
        (xm_hbm.at[0:W], ua.at[0:W, own]),
        (u_hbm.at[0:2], ua.at[W : W + 2, own]),
        (u_hbm.at[cx - 2 : cx], ua.at[SPAN + W - 1 : SPAN + W + 1, own]),
        (xp_hbm.at[0:W], ua.at[SPAN + W + 1 : 2 * SPAN, own]),
        (xm_hbm.at[W : 2 * W], dd.at[0:W, own]),
        (d_hbm.at[0 : W + 1], dd.at[W:SPAN, own]),
        (d_hbm.at[cx - W - 1 : cx], dd.at[SPAN : SPAN + W + 1, own]),
        (xp_hbm.at[W : 2 * W], dd.at[SPAN + W + 1 : 2 * SPAN, own]),
        (xm_hbm.at[2 * W : 3 * W - 1], rr.at[1:W, own]),
        (r_hbm.at[0 : W + 1], rr.at[W:SPAN, own]),
        (r_hbm.at[cx - W - 1 : cx], rr.at[SPAN : SPAN + W + 1, own]),
        (xp_hbm.at[2 * W : 3 * W - 1], rr.at[SPAN + W + 1 : 2 * SPAN - 1, own]),
        (field_hbm.at[W:8], fin.at[W:8]),
        (field_hbm.at[cx - 8 : cx - W], fin.at[8 : 16 - W]),
    ):
        copies.append(pltpu.make_async_copy(src, dst, sems.at[len(copies)]))
    for copy in copies:
        copy.start()

    rr[0] = jnp.zeros((cy + 8, nz), F32)
    rr[2 * SPAN - 1] = jnp.zeros((cy + 8, nz), F32)

    def rows(dst, plane, after, before):
        dst[plane, cy : cy + W, :] = after
        dst[plane, cy + W : cy + 2 * W, :] = before

    for i in range(W + 1):
        for base, x in ((W + i, i), (SPAN + i, cx - W - 1 + i)):
            for which, dst in enumerate((ua, dd, rr)):
                rows(dst, base, yn[which, x], yp[which, x])
    for side, base in ((0, 0), (1, SPAN + W + 1)):
        at = side * (3 * W - 1)
        for i in range(W):
            rows(ua, base + i, cn[at + i], cp[at + i])
            rows(dd, base + i, cn[at + W + i], cp[at + W + i])
        for i in range(W - 1):
            rows(rr, base + i + 1 - side, cn[at + 2 * W + i], cp[at + 2 * W + i])
    work = Plane(dd, dn, rr, kk, fbuf)
    sx = lax.axis_index("sx")
    first = (sx > 0).astype(F32)
    final = (sx < lax.axis_size("sx") - 1).astype(F32)
    for copy in copies:
        copy.wait()
    lax.fori_loop(0, dd.shape[0], lambda i, c: (work.prepare(i), c)[1], 0, unroll=2)

    src, dst = ua, ub
    for step in range(STEPS):
        last = step == STEPS - 1

        def end(side, carry, src=src, dst=dst, step=step, last=last):
            base = jnp.where(side == 0, step, SPAN + W - 1 - step)
            for i in range(3):
                work.local(src, dst, base + i)
            work.face(src, base + 1)
            for j in range(W):
                keep = None
                if not last:
                    keep = jnp.where(
                        side == 0, first if j < W - 1 - step else 1.0, final if j > step else 1.0
                    )
                target = side * (16 - W) + j if last else base + 1 + j
                work.across(src, dst, fin if last else dst, base + 1 + j, target, keep)
                if j < W - 1:
                    work.local(src, dst, base + 3 + j)
            return carry

        lax.fori_loop(0, 2, end, 0)
        if not last:
            for i in range(2):
                dst[step + W + 1 + i] = rim[4 * step + i]
                dst[SPAN + W - 2 - step + i] = rim[4 * step + 2 + i]
            src, dst = dst, src
    done = [
        pltpu.make_async_copy(fin.at[0:W], out_hbm.at[0:W], osem.at[0]),
        pltpu.make_async_copy(fin.at[16 - W : 16], out_hbm.at[cx - W : cx], osem.at[1]),
    ]
    for copy in done:
        copy.start()
    turn_over(fin, turned)
    for group in range(2):
        shear_rows(offs, turned, moved, group)

        def one(view, carry, group=group):
            def store(d, at, value):
                parts[4 * group + d, pl.ds(pl.multiple_of(8 * view, 8), 8), at] = value

            march(scene, order, moved, view, store)
            return carry

        lax.fori_loop(0, VIEWS, one, 0)
        first = group * (cx // 2 - 4)
        done.append(
            pltpu.make_async_copy(
                parts.at[4 * group : 4 * group + 4],
                all_hbm.at[first : first + 4],
                osem.at[2 + group],
            )
        )
        done[-1].start()
    for copy in done:
        copy.wait()


def outer(u, d, r, yn, yp, xm, xp, cn, cp, rim, offs, scene, order, field, parts):
    cx, cy, nz = u.shape
    wide = pltpu.VMEM((2 * SPAN, cy + 8, nz), F32)
    return pl.pallas_call(
        outer_kernel,
        out_shape=(
            jax.ShapeDtypeStruct((cx, cy, nz), F32),
            jax.ShapeDtypeStruct(parts.shape, F32),
        ),
        in_specs=[ANYWHERE] * 3 + [LOCAL] * 2 + [ANYWHERE] * 2 + [LOCAL] * 3 + [SCALARS] * 2 + [LOCAL] + [ANYWHERE] * 2,
        out_specs=(ANYWHERE, ANYWHERE),
        scratch_shapes=[wide] * 6
        + [
            pltpu.VMEM((cy + 8, nz), F32),
            pltpu.VMEM((16, cy, nz), F32),
            pltpu.VMEM((cy, 16, nz), F32),
            pltpu.VMEM((VIEWS, cy, 8, nz), F32),
            pltpu.VMEM((8, 8 * VIEWS, nz), F32),
            pltpu.SemaphoreType.DMA((14,)),
            pltpu.SemaphoreType.DMA((4,)),
        ],
        input_output_aliases={13: 0, 14: 1},
        name="outer",
    )(u, d, r, yn, yp, xm, xp, cn, cp, rim, offs, scene, order, field, parts)


def shear_rows(offs, ft, moved, group):
    depth, nz = ft.shape[0], ft.shape[2]
    blocks = nz // 128
    lane = lax.broadcasted_iota(jnp.int32, (8, 128), 1)
    lane_last = lane == 127
    zero = jnp.zeros((8, 128), F32)
    rows = slice(0, 8) if group is None else pl.ds(pl.multiple_of(8 * group, 8), 8)
    first = lax.axis_index("sy") * depth

    def shear(y, carry):
        cells = [ft[y, rows, 128 * b : 128 * b + 128] for b in range(blocks)]
        back = [pltpu.roll(c, 127, 1) for c in cells] + [zero]
        slope = [jnp.where(lane_last, back[b + 1], back[b]) - cells[b] for b in range(blocks)]
        for v in range(VIEWS):
            q = offs[v, first + y]
            n = lax.div(q, 4)
            f = (q - 4 * n).astype(F32) * 0.25
            turn = lax.rem(128 - n, 128)
            keep = lane < 128 - n
            back = [pltpu.roll(cells[b] + f * slope[b], turn, 1) for b in range(blocks)] + [zero]
            for b in range(blocks):
                moved[v, y, :, 128 * b : 128 * b + 128] = jnp.where(keep, back[b], back[b + 1])
        return carry

    lax.fori_loop(0, depth, shear, 0, unroll=8)


def march(scene, order, moved, view, store):
    depth, rows, nz = moved.shape[1], moved.shape[2], moved.shape[3]
    zero = jnp.zeros((rows, 128), F32)
    for b in range(nz // 128):
        at = slice(128 * b, 128 * b + 128)
        side = jnp.broadcast_to(order[0:1, at], (rows, 128))
        for v in range(1, VIEWS):
            side = jnp.where(view == v, jnp.broadcast_to(order[v : v + 1, at], (rows, 128)), side)
        sign = jnp.where(side == 0, -1.0, 1.0)
        rising = sign < 0.0
        light = jnp.ones((rows, 128), F32)
        sums = [zero] * BUMPS
        for y in range(depth):
            s = moved[view, y, :, at]
            bumps = []
            for i in range(BUMPS):
                t = s - scene[0, i]
                bumps.append(jnp.exp2(scene[1, i] - t * t))
            pairs = [bumps[i] + bumps[i + 1] for i in range(0, BUMPS, 2)]
            total = (pairs[0] + pairs[1]) + (pairs[2] + pairs[3])
            after = light * jnp.exp2(total * sign)
            weight = light - after
            light = after
            sums = [sums[i] + bumps[i] * weight for i in range(BUMPS)]
        inverse = 1.0 / light
        through = jnp.where(rising, light, inverse)
        scale = jnp.where(rising, 1.0, -inverse)
        channels = []
        for c in range(3):
            value = scene[2 + c, 0] * sums[0]
            for i in range(1, BUMPS):
                value = value + scene[2 + c, i] * sums[i]
            channels.append(value * scale)
        channels.append(through)
        for d in range(rows // 2):
            store(d, at, jnp.concatenate([c[2 * d : 2 * d + 2] for c in channels], axis=0))


def render_kernel(offs, scene, order, ft, out, moved):
    view = pl.program_id(1)

    @pl.when(view == 0)
    def _():
        shear_rows(offs, ft, moved, None)

    def store(d, at, value):
        out[d, :, at] = value

    march(scene, order, moved, view, store)


def render(offs, scene, order, ft, spread, count):
    cy, cx, nz = ft.shape
    cells = VIEWS * cx * cy * nz
    return pl.pallas_call(
        render_kernel,
        out_shape=jax.ShapeDtypeStruct((count, 8 * VIEWS, nz), F32),
        grid=(cx // 8, VIEWS),
        in_specs=[SCALARS] * 2
        + [
            pl.BlockSpec((VIEWS, nz), lambda i, v: (0, 0)),
            pl.BlockSpec((cy, 8, nz), lambda i, v: (0, i, 0)),
        ],
        out_specs=pl.BlockSpec((4, 8, nz), lambda i, v: (spread(i), v, 0)),
        scratch_shapes=[pltpu.VMEM((VIEWS, cy, 8, nz), F32)],
        cost_estimate=pl.CostEstimate(
            flops=60 * cells, bytes_accessed=4 * (cx * cy + count * 8 * VIEWS) * nz, transcendentals=9 * cells
        ),
        name="render",
    )(offs, scene, order, ft)


def combine_kernel(parts, order, image, trans):
    count, _, nz = parts.shape
    sub = lax.broadcasted_iota(jnp.int32, (8, nz), 0)
    for view in range(VIEWS):
        rising = jnp.broadcast_to(order[view : view + 1, :], (8, nz)) == 0
        total = jnp.zeros((8, nz), F32)
        ahead = jnp.ones((8, nz), F32)
        for source in range(count):
            block = parts[source, 8 * view : 8 * view + 8, :]
            tail = jnp.where(sub >= 6, block, 0.0)
            pair = tail + pltpu.roll(tail, 4, 0)
            light = pair + pltpu.roll(pair, 2, 0)
            total = total * jnp.where(rising, 1.0, light) + block * jnp.where(rising, ahead, 1.0)
            ahead = ahead * light
        for c in range(3):
            image[view, c] = total[2 * c : 2 * c + 2]
        trans[view] = ahead[6:8]


def combine(parts, order):
    nz = parts.shape[2]
    return pl.pallas_call(
        combine_kernel,
        out_shape=(
            jax.ShapeDtypeStruct((VIEWS, 3, 2, nz), F32),
            jax.ShapeDtypeStruct((VIEWS, 2, nz), F32),
        ),
        name="combine",
    )(parts, order)


def scene_of(u, d, r, offsets, depth_order, centres, colour, opacity):
    cx, cy, _ = u.shape
    up_y, down_y = rows_of(u, d, r)
    yp = shift(up_y, "sy", True)
    yn = shift(down_y, "sy", False)
    up_x, down_x = planes_of(u, d, r)
    xm = shift(up_x, "sx", True)
    xp = shift(down_x, "sx", False)
    cp = shift(jnp.concatenate([xm[:, cy - W :], xp[:, cy - W :]]), "sy", True)
    cn = shift(jnp.concatenate([xm[:, :W], xp[:, :W]]), "sy", False)
    level = opacity * LOG2E
    scene = jnp.concatenate([(centres * GAIN)[None], jnp.log2(level)[None], colour / level])

    field, turned, rim = inner(u, d, r, yn, yp)
    parts = render(offsets, scene, depth_order, turned, lambda i: i + 1, cx // 2)
    field, parts = outer(
        u, d, r, yn, yp, xm, xp, cn, cp, rim, offsets, scene, depth_order, field, parts
    )
    parts = lax.all_to_all(parts, "sy", split_axis=0, concat_axis=0, tiled=True)
    image, trans = combine(parts, depth_order)
    return field, image, trans


def solution(mesh):
    grid = P("sx", "sy", None)
    return jax.shard_map(
        scene_of,
        mesh=mesh,
        in_specs=(grid, grid, grid, P(), P(), P(), P(), P()),
        out_specs=(
            grid,
            P(None, None, ("sx", "sy"), None),
            P(None, ("sx", "sy"), None),
        ),
        check_vma=False,
    )
```
